32 devices in a mesh: cp: 4 (over y, x), grp: 8 (over z, core).
Axes of the slice: x: 2, y: 2, z: 4, core: 2. Of those that a mesh axis runs over, the one named last changes fastest.
Arguments:
- queries: bfloat16 [16, 512, 2048], P('grp', 'cp'), may hold values from -108 to 108
- keys: bfloat16 [16, 512, 2048], P('grp', 'cp'), may hold values from -4 to 4
- values: bfloat16 [16, 512, 2048], P('grp', 'cp'), may hold values from -6 to 6
- lengths: int32 [16], P('grp'), may hold values from 128 to 512
- frame_map: bfloat16 [2048, 2176], replicated, may hold values from -0.125 to 0.125
- proj_weight: bfloat16 [2176, 4096], P('grp', 'cp'), may hold values from -0.125 to 0.125
- head_weight: bfloat16 [4096, 256], P('cp'), may hold values from -0.375 to 0.375
- act_embed: float32 [7, 4096], P(None, 'cp'), may hold values from -0.5 to 0.5
- actions: int32 [16, 7], P('grp'), may hold values from 0 to 255
- action_mask: int32 [16, 7], P('grp'), may hold values 0 or 1
- group_ids: int32 [16], P('grp'), may hold values from 0 to 1
- rewards: float32 [16], P('grp'), may hold values from -6 to 6
Outputs:
- logprobs: float32 [16, 7], P('grp')
- grad_proj: bfloat16 [2176, 4096], P('grp', 'cp')
- grad_head: bfloat16 [4096, 256], P('cp')
The draws below stay inside these ranges and needn't reach their ends.
All inputs are finite; a program needn't handle non-finite values. No bound on the sum of `action_mask` on one device may be relied on, other than what follows from the above.
Results may differ from the reference program's by a relative error of at most 0.018.
Values may be sent and summed in bfloat16 or wider, within the bound.
A program may use at most 128 MiB of HBM per device.

```python
import math
import jax
import jax.numpy as jnp
from jax import lax

TOK_CP = 128
HEADS = 16
HD = 128
VIS = 2176
HID = 4096
NBINS = 256
NACT = 7
SEQ = 512
EPISODES = 16
NGROUPS = 2
N_CP = 4


def query_key_pair(key):
    base = jax.random.fold_in(key, 31)
    keys_key, target_key, strength_key = jax.random.split(base, 3)
    key_rows = jnp.clip(jax.random.normal(keys_key, (EPISODES, SEQ, HEADS * HD), jnp.float32), -4.0, 4.0)
    key_heads = key_rows.reshape(EPISODES, SEQ, HEADS, HD)
    targets = jax.random.randint(target_key, (EPISODES, SEQ, HEADS, 1), 0, SEQ)
    pointed = jnp.take_along_axis(key_heads, jnp.broadcast_to(targets, (EPISODES, SEQ, HEADS, HD)), axis=1)
    strength = jnp.exp(jax.random.uniform(strength_key, (EPISODES, SEQ, HEADS, 1), jnp.float32, math.log(2.0), math.log(27.0)))
    query_rows = jnp.clip(strength * pointed, -108.0, 108.0).reshape(EPISODES, SEQ, HEADS * HD)
    return (query_rows, key_rows)


def draw_queries(key, part):
    return query_key_pair(key)[0].astype(jnp.bfloat16)


def draw_keys(key, part):
    return query_key_pair(key)[1].astype(jnp.bfloat16)


def draw_values(key, part):
    base = jax.random.fold_in(key, 59)
    coeff_key, direction_key, noise_key = jax.random.split(base, 3)
    coeff = jnp.clip(jax.random.normal(coeff_key, (EPISODES, SEQ, 1), jnp.float32), -3.0, 3.0)
    direction = jnp.clip(jax.random.normal(direction_key, (EPISODES, 1, HEADS * HD), jnp.float32), -3.0, 3.0)
    noise = 0.8 * jax.random.normal(noise_key, (EPISODES, SEQ, HEADS * HD), jnp.float32)
    return jnp.clip(coeff * direction + noise, -6.0, 6.0).astype(jnp.bfloat16)


def draw_act_embed(key, part):
    base = 0.03 * jnp.clip(jax.random.normal(jax.random.fold_in(key, 47), (NACT, HID), jnp.float32), -5.0, 5.0)
    return base


def with_ends(result, key, least, largest):
    extent = result.shape
    place = [jax.random.randint(jax.random.fold_in(key, axis), (), 0, extent[axis]) for axis in range(len(extent))]
    result = result.at[tuple(place)].set(least)
    longest = extent.index(max(extent))
    place[longest] = (place[longest] + 1) % extent[longest]
    return result.at[tuple(place)].set(largest)


def shard_levels(key, extent, cuts, smallest, largest):
    level, own = 1.0, jax.random.fold_in(key, 6)
    for position, blocks in cuts:
        heights = jnp.exp(jax.random.uniform(jax.random.fold_in(own, position), (blocks,), jnp.float32, smallest / len(cuts), largest / len(cuts)))
        level = level * jnp.repeat(heights, extent[position] // blocks).reshape([-1 if axis == position else 1 for axis in range(len(extent))])
    return level


def bell_draw(own_key, dims, deviation, limit, cuts=(), held_as=jnp.bfloat16):
    values = jax.random.normal(own_key, dims, jnp.float32) * deviation
    if len(cuts) > 0:
        values = shard_levels(own_key, dims, cuts, -0.22, 0.18) * values
    return jnp.clip(values, min=-limit, max=limit).astype(held_as)


def setup_inputs(seed: int = 0) -> dict:
    key_of = jax.random.split(jax.random.key(seed), 13)
    queries = draw_queries(jax.random.fold_in(key_of[12], 71), 0)
    keys = draw_keys(jax.random.fold_in(key_of[12], 71), 0)
    values = draw_values(jax.random.fold_in(key_of[12], 71), 0)
    lengths = with_ends(jax.random.randint(key_of[3], (EPISODES,), TOK_CP * N_CP // 4, TOK_CP * N_CP + 1), jax.random.fold_in(key_of[3], 1), TOK_CP * N_CP // 4, TOK_CP * N_CP).astype(jnp.int32)
    frame_map = bell_draw(key_of[4], (HEADS * HD, VIS), (HEADS * HD) ** -0.5, 0.125)
    proj_weight = bell_draw(key_of[5], (VIS, HID), VIS ** -0.5, 0.125, ((0, 8), (1, 4)))
    head_weight = bell_draw(key_of[6], (HID, NBINS), (HID // 16) ** -0.5, 0.375, ((0, 4),))
    act_embed = draw_act_embed(jax.random.fold_in(key_of[12], 71), 0)
    actions = with_ends(jax.random.randint(key_of[8], (EPISODES, NACT), 0, NBINS), jax.random.fold_in(key_of[8], 1), 0, NBINS - 1).astype(jnp.int32)
    action_mask = with_ends((jax.random.randint(key_of[9], (EPISODES, NACT), 0, 4) < 3).astype(jnp.int32), jax.random.fold_in(key_of[9], 1), 0, 1)
    group_ids = with_ends(jax.random.randint(key_of[10], (EPISODES,), 0, NGROUPS), jax.random.fold_in(key_of[10], 1), 0, NGROUPS - 1).astype(jnp.int32)
    rewards = bell_draw(key_of[11], (EPISODES,), 1.0, 6.0, ((0, 8),), jnp.float32)
    return dict(queries=queries, keys=keys, values=values, lengths=lengths, frame_map=frame_map, proj_weight=proj_weight, head_weight=head_weight, act_embed=act_embed, actions=actions, action_mask=action_mask, group_ids=group_ids, rewards=rewards)


SQRT_HALF = 0.7071067811865476
INV_ROOT_TAU = 0.3989422804014327
NEG_LARGE = -1e+30

def gelu_exact(values_in):
    return 0.5 * values_in * (1.0 + lax.erf(values_in * SQRT_HALF))

def gelu_slope(values_in):
    return 0.5 * (1.0 + lax.erf(values_in * SQRT_HALF)) + values_in * jnp.exp(-0.5 * values_in * values_in) * INV_ROOT_TAU

def attend(query_rows, key_rows, value_rows, length):
    query_heads = query_rows.reshape(SEQ, HEADS, HD).astype(jnp.float32)
    key_heads = key_rows.reshape(SEQ, HEADS, HD).astype(jnp.float32)
    value_heads = value_rows.reshape(SEQ, HEADS, HD).astype(jnp.float32)
    scores = jnp.einsum('ihd,jhd->hij', query_heads, key_heads) / math.sqrt(HD)
    live_keys = jnp.arange(SEQ, dtype=jnp.int32) < length
    scores = jnp.where(live_keys[None, None, :], scores, NEG_LARGE)
    row_max = lax.optimization_barrier(jnp.max(scores, axis=-1, keepdims=True))
    probs = jnp.where(live_keys[None, None, :], jnp.exp(scores - row_max), 0.0)
    row_total = lax.optimization_barrier(jnp.sum(probs, axis=-1))
    weighted = jnp.einsum('hij,jhd->ihd', probs.astype(jnp.bfloat16).astype(jnp.float32), value_heads)
    output = weighted / jnp.transpose(row_total)[:, :, None]
    return output.reshape(SEQ, HEADS * HD).astype(jnp.bfloat16)

def reference(queries, keys, values, lengths, frame_map, proj_weight, head_weight, act_embed, actions, action_mask, group_ids, rewards):
    positions = jnp.arange(SEQ, dtype=jnp.int32)

    def forward(element):
        query_rows, key_rows, value_rows, length = element
        attended = attend(query_rows, key_rows, value_rows, length)
        frames = jnp.dot(attended, frame_map, preferred_element_type=jnp.float32).astype(jnp.bfloat16)
        hidden = gelu_exact(jnp.dot(frames, proj_weight, preferred_element_type=jnp.float32))
        token_mask = (positions < length).astype(jnp.float32)
        pooled = lax.optimization_barrier(jnp.sum(token_mask[:, None] * hidden, axis=0)) / length.astype(jnp.float32)
        return (frames, pooled)
    frames, pooled = lax.map(forward, (queries, keys, values, lengths))
    sum_input = pooled[:, None, :] + act_embed[None, :, :]
    head_input = sum_input.astype(jnp.bfloat16).reshape(EPISODES * NACT, HID)
    logits = jnp.dot(head_input, head_weight, preferred_element_type=jnp.float32)
    log_all = jax.nn.log_softmax(logits, axis=-1)
    bin_ids = jnp.arange(NBINS, dtype=jnp.int32)
    picked = (actions.reshape(-1)[:, None] == bin_ids[None, :]).astype(jnp.float32)
    logprobs = lax.optimization_barrier(jnp.sum(picked * log_all, axis=-1)).reshape(EPISODES, NACT)
    membership = (group_ids[:, None] == jnp.arange(NGROUPS, dtype=jnp.int32)[None, :]).astype(jnp.float32)
    group_sizes = lax.optimization_barrier(jnp.sum(membership, axis=0))
    reward_sums = lax.optimization_barrier(jnp.sum(membership * rewards[:, None], axis=0))
    squares = lax.optimization_barrier(jnp.sum(membership * (rewards * rewards)[:, None], axis=0))
    size_floor = jnp.maximum(group_sizes, 1.0)
    group_mean = reward_sums / size_floor
    variance = squares / size_floor - group_mean * group_mean
    group_scale = jnp.sqrt(jnp.maximum(variance, 1.0))
    advantage = (rewards - lax.optimization_barrier(jnp.sum(membership * group_mean[None, :], axis=1))) / lax.optimization_barrier(jnp.sum(membership * group_scale[None, :], axis=1))
    masked = action_mask.astype(jnp.float32)
    mask_total = jnp.maximum(jnp.sum(masked), 1.0)
    loss_weight = (-masked * advantage[:, None] / mask_total).reshape(-1)
    logit_grad = (loss_weight[:, None] * (picked - jnp.exp(log_all))).astype(jnp.bfloat16)
    grad_head = jnp.dot(jnp.transpose(head_input), logit_grad, preferred_element_type=jnp.float32).astype(jnp.bfloat16)
    pool_grad = lax.optimization_barrier(jnp.sum(jnp.dot(logit_grad, jnp.transpose(head_weight), preferred_element_type=jnp.float32).reshape(EPISODES, NACT, HID), axis=1))

    def accumulate(running, element):
        frame_rows, length, pull = element
        pre_act = jnp.dot(frame_rows, proj_weight, preferred_element_type=jnp.float32)
        token_mask = (positions < length).astype(jnp.float32) / length.astype(jnp.float32)
        act_grad = (token_mask[:, None] * pull[None, :] * gelu_slope(pre_act)).astype(jnp.bfloat16)
        return (running + jnp.dot(jnp.transpose(frame_rows), act_grad, preferred_element_type=jnp.float32), None)
    start_grad = jnp.zeros((VIS, HID), jnp.float32)
    grad_proj, _ = lax.scan(accumulate, start_grad, (frames, lengths, pool_grad))
    return (logprobs, grad_proj.astype(jnp.bfloat16), grad_head)
```

```python
import math

import jax
import jax.numpy as jnp
from jax import lax
from jax.experimental import pallas as pl
from jax.experimental.pallas import tpu as pltpu
from jax.sharding import PartitionSpec as P

HD = 128
ON_MESH = pl.DeviceIdType.MESH

SQRT_HALF = 0.7071067811865476
INV_ROOT_TAU = 0.3989422804014327
NEG_LARGE = -1e30


def gelu_exact(values_in):
    return 0.5 * values_in * (1.0 + lax.erf(values_in * SQRT_HALF))


def gelu_slope(values_in):
    return (
        0.5 * (1.0 + lax.erf(values_in * SQRT_HALF))
        + values_in * jnp.exp(-0.5 * values_in * values_in) * INV_ROOT_TAU
    )


def fetch_columns(proj_weight):
    return lax.all_gather(proj_weight, "grp", axis=0, tiled=True)


def attention(queries, keys, values, lengths):
    episodes_here, tokens_here, att_width = queries.shape
    head_count = att_width // HD
    query_heads = queries.reshape(episodes_here, tokens_here, head_count, HD)
    key_heads = keys.reshape(episodes_here, tokens_here, head_count, HD)
    value_heads = values.reshape(episodes_here, tokens_here, head_count, HD)
    query_all, key_all, value_all = (
        lax.all_to_all(query_heads, "cp", split_axis=2, concat_axis=1, tiled=True),
        lax.all_to_all(key_heads, "cp", split_axis=2, concat_axis=1, tiled=True),
        lax.all_to_all(value_heads, "cp", split_axis=2, concat_axis=1, tiled=True),
    )
    seq_span = query_all.shape[1]
    scores = jnp.einsum(
        "eihd,ejhd->ehij", query_all, key_all, preferred_element_type=jnp.float32
    ) / math.sqrt(HD)
    live_keys = (jnp.arange(seq_span, dtype=jnp.int32)[None, :] < lengths[:, None])[
        :, None, None, :
    ]
    scores = jnp.where(live_keys, scores, NEG_LARGE)
    row_max = jnp.max(scores, axis=-1, keepdims=True)
    probs = jnp.where(live_keys, jnp.exp(scores - row_max), 0.0)
    row_total = jnp.sum(probs, axis=-1)
    weighted = jnp.einsum(
        "ehij,ejhd->eihd", probs.astype(jnp.bfloat16), value_all, preferred_element_type=jnp.float32
    )
    output = (weighted / jnp.transpose(row_total, (0, 2, 1))[..., None]).astype(jnp.bfloat16)
    returned = lax.all_to_all(output, "cp", split_axis=1, concat_axis=2, tiled=True)
    return returned.reshape(episodes_here, tokens_here, att_width)


def remote(source, target, send_sem, recv_sem, where):
    return pltpu.make_async_remote_copy(
        src_ref=source,
        dst_ref=target,
        send_sem=send_sem,
        recv_sem=recv_sem,
        device_id=where,
        device_id_type=ON_MESH,
    )


def greet(peers):
    barrier = pltpu.get_barrier_semaphore()
    for where in peers:
        pl.semaphore_signal(barrier, inc=1, device_id=where, device_id_type=ON_MESH)
    pl.semaphore_wait(barrier, len(peers))


def exchange_kernel(
    n_cp, n_grp, logits_ref, stats_ref, logits_out, stats_out, logits_all, stats_all, sends, recvs, sends_g, recvs_g
):
    me, group = lax.axis_index("cp"), lax.axis_index("grp")
    peers = [lax.rem(me + step, n_cp) for step in range(1, n_cp)]
    peers_g = [lax.rem(group + step, n_grp) for step in range(1, n_grp)]
    greet([(peer, group) for peer in peers] + [(me, peer) for peer in peers_g])
    for step, peer in enumerate(peers):
        remote(logits_ref, logits_all.at[me], sends.at[step], recvs.at[me], (peer, group)).start()
    for step, peer in enumerate(peers_g):
        remote(stats_ref, stats_all.at[group], sends_g.at[step], recvs_g.at[group], (me, peer)).start()
    logits_all[me] = logits_ref[...]
    stats_all[group] = stats_ref[...]
    for peer in peers_g:
        remote(stats_ref, stats_all.at[peer], sends_g.at[0], recvs_g.at[peer], (me, peer)).wait_recv()
    stats_out[...] = jnp.sum(stats_all[...], axis=0)
    for peer in peers:
        remote(logits_ref, logits_all.at[peer], sends.at[0], recvs.at[peer], (peer, group)).wait_recv()
    total = logits_all[0]
    for slot in range(1, n_cp):
        total = total + logits_all[slot]
    logits_out[...] = total
    for step, peer in enumerate(peers):
        remote(logits_ref, logits_all.at[me], sends.at[step], recvs.at[me], (peer, group)).wait_send()
    for step, peer in enumerate(peers_g):
        remote(stats_ref, stats_all.at[group], sends_g.at[step], recvs_g.at[group], (me, peer)).wait_send()


def exchange(partial_logits, stats):
    n_cp, n_grp = lax.axis_size("cp"), lax.axis_size("grp")
    in_vmem = pl.BlockSpec(memory_space=pltpu.VMEM)
    dma = pltpu.SemaphoreType.DMA
    return pl.pallas_call(
        lambda *refs: exchange_kernel(n_cp, n_grp, *refs),
        out_shape=(
            jax.ShapeDtypeStruct(partial_logits.shape, jnp.float32),
            jax.ShapeDtypeStruct(stats.shape, jnp.float32),
        ),
        in_specs=[in_vmem] * 2,
        out_specs=(in_vmem,) * 2,
        scratch_shapes=[
            pltpu.VMEM((n_cp,) + partial_logits.shape, jnp.float32),
            pltpu.VMEM((n_grp,) + stats.shape, jnp.float32),
            dma((n_cp,)),
            dma((n_cp,)),
            dma((n_grp,)),
            dma((n_grp,)),
        ],
        compiler_params=pltpu.CompilerParams(collective_id=1, has_side_effects=True),
        name="exchange",
    )(partial_logits, stats)


def add_rows(target, terms):
    rows = target.shape[0]
    block = 16 if rows % 16 == 0 else 8

    def some(index, carry):
        at = pl.ds(pl.multiple_of(index * block, block), block)
        total = terms[0][at, :].astype(jnp.float32)
        for term in terms[1:]:
            total = total + term[at, :].astype(jnp.float32)
        target[at, :] = total.astype(target.dtype)
        return carry

    lax.fori_loop(0, rows // block, some, 0)


def reduce_kernel(
    n_out,
    partial,
    head_ref,
    grad_ref,
    out_ref,
    grad_head_ref,
    pair_recv,
    up_send,
    up_recv,
    down_send,
    down_recv,
    head_all,
    grad_all,
    pair_sems,
    up_sems,
    down_sems,
    head_sems,
    grad_sems,
):
    n_grp = 2 * n_out
    me, group = lax.axis_index("cp"), lax.axis_index("grp")
    place, core = group // 2, lax.rem(group, 2)
    sibling = (me, 2 * place + 1 - core)
    above, below = (me, lax.rem(group + 2, n_grp)), (me, lax.rem(group + n_grp - 2, n_grp))
    peers = [lax.rem(group + step, n_grp) for step in range(1, n_grp)]
    greet([(me, peer) for peer in peers])

    order = []
    for step in range(n_out):
        for target in (n_out - 1 - step, step):
            if target not in order:
                order.append(target)

    def pair_copy(target):
        return remote(
            partial.at[2 * target + 1 - core],
            pair_recv.at[target],
            pair_sems.at[0, target],
            pair_sems.at[1, target],
            sibling,
        )

    def up_copy(target):
        return remote(up_send.at[target], up_recv.at[target], up_sems.at[0, target], up_sems.at[1, target], above)

    def down_copy(target):
        return remote(
            down_send.at[target], down_recv.at[target], down_sems.at[0, target], down_sems.at[1, target], below
        )

    for target in order:
        pair_copy(target).start()

    def head_copies(step, owner, peer):
        return (
            remote(head_ref, head_all.at[owner], head_sems.at[0, step], head_sems.at[1, owner], (me, peer)),
            remote(grad_ref, grad_all.at[owner], grad_sems.at[0, step], grad_sems.at[1, owner], (me, peer)),
        )

    for step, peer in enumerate(peers):
        for copy in head_copies(step, group, peer):
            copy.start()
    head_all[group] = head_ref[...]
    grad_all[group] = grad_ref[...]

    for step in range(n_out):
        up_to, down_to = n_out - 1 - step, step

        @pl.when(up_to > place)
        def _():
            pair_copy(up_to).wait_recv()
            own = [partial.at[2 * up_to + core], pair_recv.at[up_to]]

            @pl.when(place == 0)
            def _():
                add_rows(up_send.at[up_to], own)

            @pl.when(place > 0)
            def _():
                up_copy(up_to).wait_recv()
                add_rows(up_send.at[up_to], own + [up_recv.at[up_to]])

            up_copy(up_to).start()

        @pl.when(down_to < place)
        def _():
            pair_copy(down_to).wait_recv()
            own = [partial.at[2 * down_to + core], pair_recv.at[down_to]]

            @pl.when(place == n_out - 1)
            def _():
                add_rows(down_send.at[down_to], own)

            @pl.when(place < n_out - 1)
            def _():
                down_copy(down_to).wait_recv()
                add_rows(down_send.at[down_to], own + [down_recv.at[down_to]])

            down_copy(down_to).start()

    for peer in peers:
        for copy in head_copies(0, peer, peer):
            copy.wait_recv()
    rows = n_grp * head_ref.shape[0]
    grad_head_ref[...] = lax.dot_general(
        head_all[...].reshape(rows, head_ref.shape[1]),
        grad_all[...].reshape(rows, grad_ref.shape[1]),
        (((0,), (0,)), ((), ())),
        preferred_element_type=jnp.float32,
    ).astype(jnp.bfloat16)

    pair_copy(place).wait_recv()
    own = [partial.at[group], pair_recv.at[place]]

    @pl.when(place == 0)
    def _():
        down_copy(place).wait_recv()
        add_rows(out_ref, own + [down_recv.at[place]])

    @pl.when(place == n_out - 1)
    def _():
        up_copy(place).wait_recv()
        add_rows(out_ref, own + [up_recv.at[place]])

    @pl.when(jnp.logical_and(place > 0, place < n_out - 1))
    def _():
        up_copy(place).wait_recv()
        down_copy(place).wait_recv()
        add_rows(out_ref, own + [up_recv.at[place], down_recv.at[place]])

    for target in range(n_out):
        pair_copy(target).wait_send()

        @pl.when(target > place)
        def _():
            up_copy(target).wait_send()

        @pl.when(target < place)
        def _():
            down_copy(target).wait_send()

    for step, peer in enumerate(peers):
        for copy in head_copies(step, group, peer):
            copy.wait_send()


def reduce_gradients(partial, head_input, logit_grad):
    n_grp = lax.axis_size("grp")
    n_out = n_grp // 2
    chunk, width = partial.shape[0] // n_grp, partial.shape[1]
    in_vmem = pl.BlockSpec(memory_space=pltpu.VMEM)
    dma = pltpu.SemaphoreType.DMA
    line = pltpu.VMEM((n_out, chunk, width), jnp.bfloat16)
    return pl.pallas_call(
        lambda *refs: reduce_kernel(n_out, *refs),
        out_shape=(
            jax.ShapeDtypeStruct((chunk, width), jnp.bfloat16),
            jax.ShapeDtypeStruct((head_input.shape[1], logit_grad.shape[1]), jnp.bfloat16),
        ),
        in_specs=[in_vmem] * 3,
        out_specs=(in_vmem,) * 2,
        scratch_shapes=[line] * 5
        + [
            pltpu.VMEM((n_grp,) + head_input.shape, jnp.bfloat16),
            pltpu.VMEM((n_grp,) + logit_grad.shape, jnp.bfloat16),
        ]
        + [dma((2, n_out))] * 3
        + [dma((2, n_grp))] * 2,
        compiler_params=pltpu.CompilerParams(
            collective_id=2, has_side_effects=True, vmem_limit_bytes=48 * 1024 * 1024
        ),
        name="reduce_gradients",
    )(partial.reshape(n_grp, chunk, width), head_input, logit_grad)


def per_device(
    queries,
    keys,
    values,
    lengths,
    frame_map,
    proj_weight,
    head_weight,
    act_embed,
    actions,
    action_mask,
    group_ids,
    rewards,
):
    episodes_here, tokens_here, att_width = queries.shape
    action_count = act_embed.shape[0]
    lengths_real = lengths.astype(jnp.float32)
    attended = attention(queries, keys, values, lengths)
    proj_cols = fetch_columns(proj_weight)
    frames = jnp.dot(
        attended.reshape(episodes_here * tokens_here, att_width),
        frame_map,
        preferred_element_type=jnp.float32,
    )
    frames = frames.astype(jnp.bfloat16).reshape(episodes_here, tokens_here, frame_map.shape[1])
    all_frames = lax.all_gather(frames, "cp", axis=1, tiled=True)
    seq_span = all_frames.shape[1]
    flat_frames = all_frames.reshape(episodes_here * seq_span, all_frames.shape[2])
    col_count = proj_cols.shape[1]
    pre_act = jnp.dot(flat_frames, proj_cols, preferred_element_type=jnp.float32).reshape(
        episodes_here, seq_span, col_count
    )
    hidden = gelu_exact(pre_act)
    token_mask = (jnp.arange(seq_span, dtype=jnp.int32)[None, :] < lengths[:, None]).astype(
        jnp.float32
    )
    pooled = jnp.sum(token_mask[:, :, None] * hidden, axis=1) / lengths_real[:, None]
    sum_input = pooled[:, None, :] + act_embed[None, :, :]
    head_input = sum_input.astype(jnp.bfloat16).reshape(episodes_here * action_count, col_count)
    partial_logits = jnp.dot(head_input, head_weight, preferred_element_type=jnp.float32)
    episodes_total = episodes_here * lax.axis_size("grp")
    group_count = max(1, episodes_total // 8)
    membership = (group_ids[:, None] == jnp.arange(group_count, dtype=jnp.int32)[None, :]).astype(
        jnp.float32
    )
    masked = action_mask.astype(jnp.float32)
    stats_row = jnp.concatenate(
        [
            jnp.sum(membership * rewards[:, None], axis=0),
            jnp.sum(membership * (rewards * rewards)[:, None], axis=0),
            jnp.sum(membership, axis=0),
            jnp.sum(masked)[None],
        ]
    )
    lanes = -(-stats_row.shape[0] // 128) * 128
    stats_row = jnp.pad(stats_row, (0, lanes - stats_row.shape[0]))
    logits, stats = exchange(partial_logits, jnp.broadcast_to(stats_row[None, :], (8, lanes)))
    reward_sums = stats[0, :group_count]
    squares = stats[0, group_count : 2 * group_count]
    group_sizes = stats[0, 2 * group_count : 3 * group_count]
    mask_total = stats[0, 3 * group_count]
    log_all = jax.nn.log_softmax(logits, axis=-1)
    bin_ids = jnp.arange(head_weight.shape[1], dtype=jnp.int32)
    picked = (actions.reshape(-1)[:, None] == bin_ids[None, :]).astype(jnp.float32)
    logprobs = jnp.sum(picked * log_all, axis=-1).reshape(episodes_here, action_count)
    size_floor = jnp.maximum(group_sizes, 1.0)
    group_mean = reward_sums / size_floor
    variance = squares / size_floor - group_mean * group_mean
    group_scale = jnp.sqrt(jnp.maximum(variance, 1.0))
    advantage = (rewards - jnp.sum(membership * group_mean[None, :], axis=1)) / jnp.sum(
        membership * group_scale[None, :], axis=1
    )
    loss_weight = (-masked * advantage[:, None] / jnp.maximum(mask_total, 1.0)).reshape(-1)
    logit_grad = (loss_weight[:, None] * (picked - jnp.exp(log_all))).astype(jnp.bfloat16)
    pull_back = lax.dot_general(
        logit_grad, head_weight, (((1,), (1,)), ((), ())), preferred_element_type=jnp.float32
    )
    pool_grad = jnp.sum(pull_back.reshape(episodes_here, action_count, col_count), axis=1)
    scaled_mask = token_mask / lengths_real[:, None]
    act_grad = (scaled_mask[:, :, None] * pool_grad[:, None, :] * gelu_slope(pre_act)).astype(
        jnp.bfloat16
    )
    act_flat = act_grad.reshape(episodes_here * seq_span, col_count)
    partial_proj = lax.dot_general(
        flat_frames, act_flat, (((0,), (0,)), ((), ())), preferred_element_type=jnp.float32
    ).astype(jnp.bfloat16)
    spare = -head_input.shape[0] % 16
    grad_proj, grad_head = reduce_gradients(
        partial_proj,
        jnp.pad(head_input, ((0, spare), (0, 0))),
        jnp.pad(logit_grad, ((0, spare), (0, 0))),
    )
    return (logprobs, grad_proj, grad_head)


def solution(mesh):
    in_specs = (
        P("grp", "cp", None),
        P("grp", "cp", None),
        P("grp", "cp", None),
        P("grp"),
        P(),
        P("grp", "cp"),
        P("cp", None),
        P(None, "cp"),
        P("grp", None),
        P("grp", None),
        P("grp"),
        P("grp"),
    )
    out_specs = (P("grp", None), P("grp", "cp"), P("cp", None))
    return jax.shard_map(
        per_device, mesh=mesh, in_specs=in_specs, out_specs=out_specs, check_vma=False
    )
```

```python
import math

import jax
import jax.numpy as jnp
from jax import lax
from jax.experimental import pallas as pl
from jax.experimental.pallas import tpu as pltpu
from jax.sharding import PartitionSpec as P

HD = 128
ON_MESH = pl.DeviceIdType.MESH

SQRT_HALF = 0.7071067811865476
INV_ROOT_TAU = 0.3989422804014327
NEG_LARGE = -1e30


def gelu_exact(values_in):
    return 0.5 * values_in * (1.0 + lax.erf(values_in * SQRT_HALF))


def gelu_slope(values_in):
    return (
        0.5 * (1.0 + lax.erf(values_in * SQRT_HALF))
        + values_in * jnp.exp(-0.5 * values_in * values_in) * INV_ROOT_TAU
    )


def remote(source, target, send_sem, recv_sem, where):
    return pltpu.make_async_remote_copy(
        src_ref=source,
        dst_ref=target,
        send_sem=send_sem,
        recv_sem=recv_sem,
        device_id=where,
        device_id_type=ON_MESH,
    )


def greet(peers):
    barrier = pltpu.get_barrier_semaphore()
    for where in peers:
        pl.semaphore_signal(barrier, inc=1, device_id=where, device_id_type=ON_MESH)
    pl.semaphore_wait(barrier, len(peers))


def exchange_kernel(
    n_cp, n_grp, logits_ref, stats_ref, logits_out, stats_out, logits_all, stats_all, sends, recvs, sends_g, recvs_g
):
    me, group = lax.axis_index("cp"), lax.axis_index("grp")
    peers = [lax.rem(me + step, n_cp) for step in range(1, n_cp)]
    peers_g = [lax.rem(group + step, n_grp) for step in range(1, n_grp)]
    greet([(peer, group) for peer in peers] + [(me, peer) for peer in peers_g])
    for step, peer in enumerate(peers):
        remote(logits_ref, logits_all.at[me], sends.at[step], recvs.at[me], (peer, group)).start()
    for step, peer in enumerate(peers_g):
        remote(stats_ref, stats_all.at[group], sends_g.at[step], recvs_g.at[group], (me, peer)).start()
    logits_all[me] = logits_ref[...]
    stats_all[group] = stats_ref[...]
    for peer in peers_g:
        remote(stats_ref, stats_all.at[peer], sends_g.at[0], recvs_g.at[peer], (me, peer)).wait_recv()
    stats_out[...] = jnp.sum(stats_all[...], axis=0)
    for peer in peers:
        remote(logits_ref, logits_all.at[peer], sends.at[0], recvs.at[peer], (peer, group)).wait_recv()
    total = logits_all[0]
    for slot in range(1, n_cp):
        total = total + logits_all[slot]
    logits_out[...] = total
    for step, peer in enumerate(peers):
        remote(logits_ref, logits_all.at[me], sends.at[step], recvs.at[me], (peer, group)).wait_send()
    for step, peer in enumerate(peers_g):
        remote(stats_ref, stats_all.at[group], sends_g.at[step], recvs_g.at[group], (me, peer)).wait_send()


def exchange(partial_logits, stats):
    n_cp, n_grp = lax.axis_size("cp"), lax.axis_size("grp")
    in_vmem = pl.BlockSpec(memory_space=pltpu.VMEM)
    dma = pltpu.SemaphoreType.DMA
    return pl.pallas_call(
        lambda *refs: exchange_kernel(n_cp, n_grp, *refs),
        out_shape=(
            jax.ShapeDtypeStruct(partial_logits.shape, jnp.float32),
            jax.ShapeDtypeStruct(stats.shape, jnp.float32),
        ),
        in_specs=[in_vmem] * 2,
        out_specs=(in_vmem,) * 2,
        scratch_shapes=[
            pltpu.VMEM((n_cp,) + partial_logits.shape, jnp.float32),
            pltpu.VMEM((n_grp,) + stats.shape, jnp.float32),
            dma((n_cp,)),
            dma((n_cp,)),
            dma((n_grp,)),
            dma((n_grp,)),
        ],
        compiler_params=pltpu.CompilerParams(collective_id=1, has_side_effects=True),
        name="exchange",
    )(partial_logits, stats)


def add_rows(target, terms):
    rows = target.shape[0]
    block = 16 if rows % 16 == 0 else 8

    def some(index, carry):
        at = pl.ds(pl.multiple_of(index * block, block), block)
        total = terms[0][at, :].astype(jnp.float32)
        for term in terms[1:]:
            total = total + term[at, :].astype(jnp.float32)
        target[at, :] = total.astype(target.dtype)
        return carry

    lax.fori_loop(0, rows // block, some, 0)


def reduce_kernel(
    n_out,
    partial,
    head_ref,
    grad_ref,
    out_ref,
    grad_head_ref,
    pair_recv,
    up_send,
    up_recv,
    down_send,
    down_recv,
    head_all,
    grad_all,
    pair_sems,
    up_sems,
    down_sems,
    head_sems,
    grad_sems,
):
    n_grp = 2 * n_out
    me, group = lax.axis_index("cp"), lax.axis_index("grp")
    place, core = group // 2, lax.rem(group, 2)
    sibling = (me, 2 * place + 1 - core)
    above, below = (me, lax.rem(group + 2, n_grp)), (me, lax.rem(group + n_grp - 2, n_grp))
    peers = [lax.rem(group + step, n_grp) for step in range(1, n_grp)]
    greet([(me, peer) for peer in peers])

    order = []
    for step in range(n_out):
        for target in (n_out - 1 - step, step):
            if target not in order:
                order.append(target)

    def pair_copy(target):
        return remote(
            partial.at[2 * target + 1 - core],
            pair_recv.at[target],
            pair_sems.at[0, target],
            pair_sems.at[1, target],
            sibling,
        )

    def up_copy(target):
        return remote(up_send.at[target], up_recv.at[target], up_sems.at[0, target], up_sems.at[1, target], above)

    def down_copy(target):
        return remote(
            down_send.at[target], down_recv.at[target], down_sems.at[0, target], down_sems.at[1, target], below
        )

    for target in order:
        pair_copy(target).start()

    def head_copies(step, owner, peer):
        return (
            remote(head_ref, head_all.at[owner], head_sems.at[0, step], head_sems.at[1, owner], (me, peer)),
            remote(grad_ref, grad_all.at[owner], grad_sems.at[0, step], grad_sems.at[1, owner], (me, peer)),
        )

    for step, peer in enumerate(peers):
        for copy in head_copies(step, group, peer):
            copy.start()
    head_all[group] = head_ref[...]
    grad_all[group] = grad_ref[...]

    for step in range(n_out):
        up_to, down_to = n_out - 1 - step, step

        @pl.when(up_to > place)
        def _():
            pair_copy(up_to).wait_recv()
            own = [partial.at[2 * up_to + core], pair_recv.at[up_to]]

            @pl.when(place == 0)
            def _():
                add_rows(up_send.at[up_to], own)

            @pl.when(place > 0)
            def _():
                up_copy(up_to).wait_recv()
                add_rows(up_send.at[up_to], own + [up_recv.at[up_to]])

            up_copy(up_to).start()

        @pl.when(down_to < place)
        def _():
            pair_copy(down_to).wait_recv()
            own = [partial.at[2 * down_to + core], pair_recv.at[down_to]]

            @pl.when(place == n_out - 1)
            def _():
                add_rows(down_send.at[down_to], own)

            @pl.when(place < n_out - 1)
            def _():
                down_copy(down_to).wait_recv()
                add_rows(down_send.at[down_to], own + [down_recv.at[down_to]])

            down_copy(down_to).start()

    for peer in peers:
        for copy in head_copies(0, peer, peer):
            copy.wait_recv()
    rows = n_grp * head_ref.shape[0]
    grad_head_ref[...] = lax.dot_general(
        head_all[...].reshape(rows, head_ref.shape[1]),
        grad_all[...].reshape(rows, grad_ref.shape[1]),
        (((0,), (0,)), ((), ())),
        preferred_element_type=jnp.float32,
    ).astype(jnp.bfloat16)

    pair_copy(place).wait_recv()
    own = [partial.at[group], pair_recv.at[place]]

    @pl.when(place == 0)
    def _():
        down_copy(place).wait_recv()
        add_rows(out_ref, own + [down_recv.at[place]])

    @pl.when(place == n_out - 1)
    def _():
        up_copy(place).wait_recv()
        add_rows(out_ref, own + [up_recv.at[place]])

    @pl.when(jnp.logical_and(place > 0, place < n_out - 1))
    def _():
        up_copy(place).wait_recv()
        down_copy(place).wait_recv()
        add_rows(out_ref, own + [up_recv.at[place], down_recv.at[place]])

    for target in range(n_out):
        pair_copy(target).wait_send()

        @pl.when(target > place)
        def _():
            up_copy(target).wait_send()

        @pl.when(target < place)
        def _():
            down_copy(target).wait_send()

    for step, peer in enumerate(peers):
        for copy in head_copies(step, group, peer):
            copy.wait_send()


def reduce_gradients(partial, head_input, logit_grad):
    n_grp = lax.axis_size("grp")
    n_out = n_grp // 2
    chunk, width = partial.shape[0] // n_grp, partial.shape[1]
    in_vmem = pl.BlockSpec(memory_space=pltpu.VMEM)
    dma = pltpu.SemaphoreType.DMA
    line = pltpu.VMEM((n_out, chunk, width), jnp.bfloat16)
    return pl.pallas_call(
        lambda *refs: reduce_kernel(n_out, *refs),
        out_shape=(
            jax.ShapeDtypeStruct((chunk, width), jnp.bfloat16),
            jax.ShapeDtypeStruct((head_input.shape[1], logit_grad.shape[1]), jnp.bfloat16),
        ),
        in_specs=[in_vmem] * 3,
        out_specs=(in_vmem,) * 2,
        scratch_shapes=[line] * 5
        + [
            pltpu.VMEM((n_grp,) + head_input.shape, jnp.bfloat16),
            pltpu.VMEM((n_grp,) + logit_grad.shape, jnp.bfloat16),
        ]
        + [dma((2, n_out))] * 3
        + [dma((2, n_grp))] * 2,
        compiler_params=pltpu.CompilerParams(
            collective_id=2, has_side_effects=True, vmem_limit_bytes=48 * 1024 * 1024
        ),
        name="reduce_gradients",
    )(partial.reshape(n_grp, chunk, width), head_input, logit_grad)


def front_kernel(
    n_cp,
    n_out,
    length_ref,
    query_ref,
    key_ref,
    value_ref,
    map_ref,
    shard_ref,
    frames_ref,
    columns_ref,
    heads_all,
    blocks,
    map_held,
    total,
    local_sems,
    swap_send,
    swap_recv,
    block_send,
    block_recv,
    shard_send,
    shard_recv,
    pass_send,
    pass_recv,
):
    episodes, tokens, _ = query_ref.shape
    width = blocks.shape[2]
    seq = tokens * n_cp
    n_grp = 2 * n_out
    me, group = lax.axis_index("cp"), lax.axis_index("grp")
    place, core = group // 2, lax.rem(group, 2)
    sibling = 2 * place + 1 - core
    square = n_cp == 4
    if square:
        row_peer = me + 1 - 2 * lax.rem(me, 2)
        col_peer = lax.rem(me + 2, 4)
        far_peer = lax.rem(row_peer + 2, 4)
        peers = [far_peer, row_peer, col_peer]
    else:
        peers = [lax.rem(me + step, n_cp) for step in range(1, n_cp)]
    lines = [2 * lax.rem(place + step, n_out) + core for step in range(1, n_out)]

    map_copy = pltpu.make_async_copy(map_ref, map_held, local_sems.at[0])
    map_copy.start()
    keep_copy = pltpu.make_async_copy(shard_ref, columns_ref.at[group], local_sems.at[1])
    keep_copy.start()

    def my_copy(tensor, source, episode):
        return pltpu.make_async_copy(
            source.at[episode, :, pl.ds(pl.multiple_of(me * width, 128), width)],
            heads_all.at[tensor, episode, pl.ds(pl.multiple_of(me * tokens, 8), tokens), :],
            local_sems.at[2 + tensor * episodes + episode],
        )

    def swap_copy(tensor, source, episode, step, owner, peer):
        return remote(
            source.at[episode, :, pl.ds(pl.multiple_of(peer * width, 128), width)],
            heads_all.at[tensor, episode, pl.ds(pl.multiple_of(owner * tokens, 8), tokens), :],
            swap_send.at[tensor, episode, step],
            swap_recv.at[tensor, episode, owner],
            (peer, group),
        )

    sources = (query_ref, key_ref, value_ref)
    for episode in range(episodes):
        for tensor, source in enumerate(sources):
            my_copy(tensor, source, episode).start()
    greet([(peer, group) for peer in peers] + [(me, peer) for peer in lines] + [(me, sibling)])
    for episode in range(episodes):
        for tensor, source in enumerate(sources):
            for step, peer in enumerate(peers):
                swap_copy(tensor, source, episode, step, me, peer).start()

    def shard_copy(step, owner, peer):
        return remote(shard_ref, columns_ref.at[owner], shard_send.at[step], shard_recv.at[owner], (me, peer))

    def pass_copy(step, owner, source):
        return remote(source, columns_ref.at[owner], pass_send.at[step], pass_recv.at[owner], (me, sibling))

    for step, peer in reversed(list(enumerate(lines))):
        shard_copy(step, group, peer).start()
    pass_copy(n_out - 1, group, shard_ref).start()

    def rows_of(owner, episode, first, count):
        return blocks.at[owner, pl.ds(episode * seq + first, count), :]

    def block_copy(episode, step, owner, peer, first, count, part):
        return remote(
            rows_of(owner, episode, first, count),
            rows_of(owner, episode, first, count),
            block_send.at[episode, step],
            block_recv.at[episode, owner, part],
            (peer, group),
        )

    strip = min(seq, 256)

    def attend(episode):
        live = lax.broadcasted_iota(jnp.int32, (strip, seq), 1) < length_ref[episode]

        def one_head(head, carry):
            at = pl.ds(pl.multiple_of(head * HD, HD), HD)
            key_head = heads_all[1, episode, :, at]
            value_head = heads_all[2, episode, :, at]
            for first in range(0, seq, strip):
                query_head = heads_all[0, episode, first : first + strip, at]
                scores = lax.dot_general(
                    query_head, key_head, (((1,), (1,)), ((), ())), preferred_element_type=jnp.float32
                )
                scores = jnp.where(live, scores * (1.0 / math.sqrt(HD)), NEG_LARGE)
                probs = jnp.exp(scores - jnp.max(scores, axis=1, keepdims=True))
                row_total = jnp.sum(probs, axis=1, keepdims=True)
                weighted = jnp.dot(probs.astype(jnp.bfloat16), value_head, preferred_element_type=jnp.float32)
                blocks[me, episode * seq + first : episode * seq + first + strip, at] = (
                    weighted / row_total
                ).astype(jnp.bfloat16)
            return carry

        lax.fori_loop(0, width // HD, one_head, 0)

    def add_frames(episode, owner, opens, closes):
        tall = min(seq, 512)
        whole, spare = divmod(frames_ref.shape[2], 256)
        depth = pl.ds(pl.multiple_of(owner * width, 128), width)

        def one_tile(first, at):
            rows = pl.ds(episode * seq + first, tall)
            part = jnp.dot(blocks[owner, rows, :], map_held[depth, at], preferred_element_type=jnp.float32)
            if not opens:
                part = part + total[rows, at]
            if closes:
                frames_ref[episode, first : first + tall, at] = part.astype(jnp.bfloat16)
            else:
                total[rows, at] = part

        for first in range(0, seq, tall):

            def step(index, carry):
                one_tile(first, pl.ds(pl.multiple_of(index * 256, 256), 256))
                return carry

            lax.fori_loop(0, whole, step, 0)
            if spare:
                one_tile(first, pl.ds(whole * 256, spare))

    for episode in range(episodes):
        for tensor, source in enumerate(sources):
            my_copy(tensor, source, episode).wait()
            for peer in peers:
                swap_copy(tensor, source, episode, 0, peer, peer).wait_recv()
        attend(episode)
        if square:
            block_copy(episode, 0, me, row_peer, 0, seq, 0).start()
            block_copy(episode, 1, me, col_peer, 0, seq, 0).start()
        else:
            for step, peer in enumerate(peers):
                block_copy(episode, step, me, peer, 0, seq, 0).start()
        if episode == 0:
            map_copy.wait()
        add_frames(episode, me, True, False)

    def forward_shards():
        for step, peer in enumerate(lines):
            shard_copy(step, peer, peer).wait_recv()
            pass_copy(step, peer, columns_ref.at[peer]).start()

    half = seq // 2
    if square:
        for episode in range(episodes):
            block_copy(episode, 0, row_peer, row_peer, 0, seq, 0).wait_recv()
            block_copy(episode, 2, row_peer, col_peer, 0, half, 0).start()
            block_copy(episode, 1, col_peer, col_peer, 0, seq, 0).wait_recv()
            block_copy(episode, 3, col_peer, row_peer, half, half, 1).start()
            add_frames(episode, row_peer, False, False)
            add_frames(episode, col_peer, False, False)
        forward_shards()
        for episode in range(episodes):
            block_copy(episode, 2, far_peer, col_peer, 0, half, 0).wait_recv()
            block_copy(episode, 3, far_peer, row_peer, half, half, 1).wait_recv()
            add_frames(episode, far_peer, False, True)
    else:
        for episode in range(episodes):
            for step, peer in enumerate(peers):
                block_copy(episode, step, peer, peer, 0, seq, 0).wait_recv()
                add_frames(episode, peer, False, step == len(peers) - 1)
        forward_shards()

    for step, peer in enumerate(lines):
        pass_copy(step, peer + 1 - 2 * core, columns_ref.at[peer]).wait_recv()
    pass_copy(n_out - 1, sibling, shard_ref).wait_recv()
    keep_copy.wait()
    for episode in range(episodes):
        for tensor, source in enumerate(sources):
            for step, peer in enumerate(peers):
                swap_copy(tensor, source, episode, step, me, peer).wait_send()
        if square:
            block_copy(episode, 0, me, row_peer, 0, seq, 0).wait_send()
            block_copy(episode, 1, me, col_peer, 0, seq, 0).wait_send()
            block_copy(episode, 2, row_peer, col_peer, 0, half, 0).wait_send()
            block_copy(episode, 3, col_peer, row_peer, half, half, 1).wait_send()
        else:
            for step, peer in enumerate(peers):
                block_copy(episode, step, me, peer, 0, seq, 0).wait_send()
    for step, peer in enumerate(lines):
        shard_copy(step, group, peer).wait_send()
        pass_copy(step, peer, columns_ref.at[peer]).wait_send()
    pass_copy(n_out - 1, group, shard_ref).wait_send()


def front(queries, keys, values, lengths, frame_map, proj_weight):
    n_cp, n_grp = lax.axis_size("cp"), lax.axis_size("grp")
    n_out = n_grp // 2
    episodes, tokens, att_width = queries.shape
    seq, width = tokens * n_cp, att_width // n_cp
    chunk, cols = proj_weight.shape
    features = frame_map.shape[1]
    anywhere = pl.BlockSpec(memory_space=pl.ANY)
    in_vmem = pl.BlockSpec(memory_space=pltpu.VMEM)
    dma = pltpu.SemaphoreType.DMA
    frames, columns = pl.pallas_call(
        lambda *refs: front_kernel(n_cp, n_out, *refs),
        out_shape=(
            jax.ShapeDtypeStruct((episodes, seq, features), jnp.bfloat16),
            jax.ShapeDtypeStruct((n_grp, chunk, cols), jnp.bfloat16),
        ),
        in_specs=[pl.BlockSpec(memory_space=pltpu.SMEM)] + [anywhere] * 4 + [in_vmem],
        out_specs=(in_vmem, anywhere),
        scratch_shapes=[
            pltpu.VMEM((3, episodes, seq, width), jnp.bfloat16),
            pltpu.VMEM((n_cp, episodes * seq, width), jnp.bfloat16),
            pltpu.VMEM(frame_map.shape, jnp.bfloat16),
            pltpu.VMEM((episodes * seq, features), jnp.float32),
            dma((2 + 3 * episodes,)),
            dma((3, episodes, n_cp)),
            dma((3, episodes, n_cp)),
            dma((episodes, max(n_cp, 4))),
            dma((episodes, n_cp, 2)),
            dma((n_out,)),
            dma((n_grp,)),
            dma((n_out,)),
            dma((n_grp,)),
        ],
        compiler_params=pltpu.CompilerParams(
            collective_id=3, has_side_effects=True, vmem_limit_bytes=60 * 1024 * 1024
        ),
        name="front",
    )(lengths, queries, keys, values, frame_map, proj_weight)
    return frames, columns.reshape(n_grp * chunk, cols)


def per_device(
    queries,
    keys,
    values,
    lengths,
    frame_map,
    proj_weight,
    head_weight,
    act_embed,
    actions,
    action_mask,
    group_ids,
    rewards,
):
    episodes_here, tokens_here, att_width = queries.shape
    action_count = act_embed.shape[0]
    lengths_real = lengths.astype(jnp.float32)
    all_frames, proj_cols = front(queries, keys, values, lengths, frame_map, proj_weight)
    seq_span = all_frames.shape[1]
    flat_frames = all_frames.reshape(episodes_here * seq_span, all_frames.shape[2])
    col_count = proj_cols.shape[1]
    pre_act = jnp.dot(flat_frames, proj_cols, preferred_element_type=jnp.float32).reshape(
        episodes_here, seq_span, col_count
    )
    hidden = gelu_exact(pre_act)
    token_mask = (jnp.arange(seq_span, dtype=jnp.int32)[None, :] < lengths[:, None]).astype(
        jnp.float32
    )
    pooled = jnp.sum(token_mask[:, :, None] * hidden, axis=1) / lengths_real[:, None]
    sum_input = pooled[:, None, :] + act_embed[None, :, :]
    head_input = sum_input.astype(jnp.bfloat16).reshape(episodes_here * action_count, col_count)
    partial_logits = jnp.dot(head_input, head_weight, preferred_element_type=jnp.float32)
    episodes_total = episodes_here * lax.axis_size("grp")
    group_count = max(1, episodes_total // 8)
    membership = (group_ids[:, None] == jnp.arange(group_count, dtype=jnp.int32)[None, :]).astype(
        jnp.float32
    )
    masked = action_mask.astype(jnp.float32)
    stats_row = jnp.concatenate(
        [
            jnp.sum(membership * rewards[:, None], axis=0),
            jnp.sum(membership * (rewards * rewards)[:, None], axis=0),
            jnp.sum(membership, axis=0),
            jnp.sum(masked)[None],
        ]
    )
    lanes = -(-stats_row.shape[0] // 128) * 128
    stats_row = jnp.pad(stats_row, (0, lanes - stats_row.shape[0]))
    logits, stats = exchange(partial_logits, jnp.broadcast_to(stats_row[None, :], (8, lanes)))
    reward_sums = stats[0, :group_count]
    squares = stats[0, group_count : 2 * group_count]
    group_sizes = stats[0, 2 * group_count : 3 * group_count]
    mask_total = stats[0, 3 * group_count]
    log_all = jax.nn.log_softmax(logits, axis=-1)
    bin_ids = jnp.arange(head_weight.shape[1], dtype=jnp.int32)
    picked = (actions.reshape(-1)[:, None] == bin_ids[None, :]).astype(jnp.float32)
    logprobs = jnp.sum(picked * log_all, axis=-1).reshape(episodes_here, action_count)
    size_floor = jnp.maximum(group_sizes, 1.0)
    group_mean = reward_sums / size_floor
    variance = squares / size_floor - group_mean * group_mean
    group_scale = jnp.sqrt(jnp.maximum(variance, 1.0))
    advantage = (rewards - jnp.sum(membership * group_mean[None, :], axis=1)) / jnp.sum(
        membership * group_scale[None, :], axis=1
    )
    loss_weight = (-masked * advantage[:, None] / jnp.maximum(mask_total, 1.0)).reshape(-1)
    logit_grad = (loss_weight[:, None] * (picked - jnp.exp(log_all))).astype(jnp.bfloat16)
    pull_back = lax.dot_general(
        logit_grad, head_weight, (((1,), (1,)), ((), ())), preferred_element_type=jnp.float32
    )
    pool_grad = jnp.sum(pull_back.reshape(episodes_here, action_count, col_count), axis=1)
    scaled_mask = token_mask / lengths_real[:, None]
    act_grad = (scaled_mask[:, :, None] * pool_grad[:, None, :] * gelu_slope(pre_act)).astype(
        jnp.bfloat16
    )
    act_flat = act_grad.reshape(episodes_here * seq_span, col_count)
    partial_proj = lax.dot_general(
        flat_frames, act_flat, (((0,), (0,)), ((), ())), preferred_element_type=jnp.float32
    ).astype(jnp.bfloat16)
    spare = -head_input.shape[0] % 16
    grad_proj, grad_head = reduce_gradients(
        partial_proj,
        jnp.pad(head_input, ((0, spare), (0, 0))),
        jnp.pad(logit_grad, ((0, spare), (0, 0))),
    )
    return (logprobs, grad_proj, grad_head)


def solution(mesh):
    in_specs = (
        P("grp", "cp", None),
        P("grp", "cp", None),
        P("grp", "cp", None),
        P("grp"),
        P(),
        P("grp", "cp"),
        P("cp", None),
        P(None, "cp"),
        P("grp", None),
        P("grp", None),
        P("grp"),
        P("grp"),
    )
    out_specs = (P("grp", None), P("grp", "cp"), P("cp", None))
    return jax.shard_map(
        per_device, mesh=mesh, in_specs=in_specs, out_specs=out_specs, check_vma=False
    )
```

```python
import math

import jax
import jax.numpy as jnp
from jax import lax
from jax.experimental import pallas as pl
from jax.experimental.pallas import tpu as pltpu
from jax.sharding import PartitionSpec as P

HD = 128
ON_MESH = pl.DeviceIdType.MESH

SQRT_HALF = 0.7071067811865476
INV_ROOT_TAU = 0.3989422804014327
NEG_LARGE = -1e30


def gelu_exact(values_in):
    return 0.5 * values_in * (1.0 + lax.erf(values_in * SQRT_HALF))


def gelu_slope(values_in):
    return (
        0.5 * (1.0 + lax.erf(values_in * SQRT_HALF))
        + values_in * jnp.exp(-0.5 * values_in * values_in) * INV_ROOT_TAU
    )


def remote(source, target, send_sem, recv_sem, where):
    return pltpu.make_async_remote_copy(
        src_ref=source,
        dst_ref=target,
        send_sem=send_sem,
        recv_sem=recv_sem,
        device_id=where,
        device_id_type=ON_MESH,
    )


def greet(peers):
    barrier = pltpu.get_barrier_semaphore()
    for where in peers:
        pl.semaphore_signal(barrier, inc=1, device_id=where, device_id_type=ON_MESH)
    pl.semaphore_wait(barrier, len(peers))


def tail_kernel(
    n_cp,
    n_out,
    group_count,
    action_ref,
    mask_ref,
    id_ref,
    reward_ref,
    frames_ref,
    slope_ref,
    head_ref,
    weight_ref,
    logprob_ref,
    out_ref,
    grad_head_ref,
    logits_send,
    logits_all,
    stats_send,
    stats_all,
    head_all,
    grad_send,
    grad_all,
    pulls,
    moments,
    pair_send,
    pair_recv,
    up_send,
    up_recv,
    down_send,
    down_recv,
    logits_sems,
    stats_sems,
    head_sems,
    grad_sems,
    pair_sems,
    up_sems,
    down_sems,
):
    episodes, action_count = action_ref.shape
    rows, _ = head_ref.shape
    bins = weight_ref.shape[1]
    seq = frames_ref.shape[1]
    chunk, width = out_ref.shape
    parts, span = pair_send.shape[1], pair_send.shape[3]
    n_grp = 2 * n_out
    me, group = lax.axis_index("cp"), lax.axis_index("grp")
    place, core = group // 2, lax.rem(group, 2)
    sibling = (me, 2 * place + 1 - core)
    above, below = (me, lax.rem(group + 2, n_grp)), (me, lax.rem(group + n_grp - 2, n_grp))
    peers = [lax.rem(me + step, n_cp) for step in range(1, n_cp)]
    peers_g = [lax.rem(group + step, n_grp) for step in range(1, n_grp)]

    def to_all(send, everyone, sems, step, owner, where):
        return remote(send, everyone.at[owner], sems.at[0, step], sems.at[1, owner], where)

    lane = lax.broadcasted_iota(jnp.int32, (8, 128), 1)
    stats = jnp.zeros((8, 128), jnp.float32)
    for episode in range(episodes):
        reward, member = reward_ref[episode], id_ref[episode]
        stats = stats + jnp.where(lane == member, reward, 0.0)
        stats = stats + jnp.where(lane == group_count + member, reward * reward, 0.0)
        stats = stats + jnp.where(lane == 2 * group_count + member, 1.0, 0.0)
        for action in range(action_count):
            valid = mask_ref[episode, action].astype(jnp.float32)
            stats = stats + jnp.where(lane == 3 * group_count, valid, 0.0)
    stats_send[...] = stats
    stats_all[group] = stats
    partial = jnp.dot(head_ref[...], weight_ref[...], preferred_element_type=jnp.float32)
    logits_send[...] = partial
    logits_all[me] = partial
    head_all[group] = head_ref[...]

    greet([(peer, group) for peer in peers] + [(me, peer) for peer in peers_g])
    for step, peer in enumerate(peers):
        to_all(logits_send, logits_all, logits_sems, step, me, (peer, group)).start()
    for step, peer in enumerate(peers_g):
        to_all(stats_send, stats_all, stats_sems, step, group, (me, peer)).start()
    for step, peer in enumerate(peers_g):
        to_all(head_ref, head_all, head_sems, step, group, (me, peer)).start()

    features = frames_ref.shape[2]
    whole, spare = divmod(features, 256)

    def moment(episode, at, down):
        moments[episode, down, :] = lax.dot_general(
            frames_ref[episode, :, at],
            slope_ref[episode],
            (((0,), (0,)), ((), ())),
            preferred_element_type=jnp.float32,
        )

    for episode in range(episodes):

        def one_tile(index, carry):
            at = pl.ds(pl.multiple_of(index * 256, 256), 256)
            moment(episode, at, at)
            return carry

        lax.fori_loop(0, whole, one_tile, 0)
        if spare:
            moment(episode, pl.ds(whole * 256, spare), pl.ds(whole * 256, spare))

    for peer in peers:
        to_all(logits_send, logits_all, logits_sems, 0, peer, (peer, group)).wait_recv()
    logits = logits_all[0]
    for slot in range(1, n_cp):
        logits = logits + logits_all[slot]
    for peer in peers_g:
        to_all(stats_send, stats_all, stats_sems, 0, peer, (me, peer)).wait_recv()
    stats = jnp.sum(stats_all[...], axis=0)[0:1]
    lane = lane[0:1]

    def entry(index):
        return jnp.sum(jnp.where(lane == index, stats, 0.0), axis=1, keepdims=True)

    mask_total = jnp.maximum(entry(3 * group_count), 1.0)
    row = lax.broadcasted_iota(jnp.int32, (rows, 1), 0)
    chosen = jnp.zeros((rows, 1), jnp.int32)
    loss_weight = jnp.zeros((rows, 1), jnp.float32)
    for episode in range(episodes):
        member = id_ref[episode]
        size = jnp.maximum(entry(2 * group_count + member), 1.0)
        mean = entry(member) / size
        variance = entry(group_count + member) / size - mean * mean
        advantage = (reward_ref[episode] - mean) / jnp.sqrt(jnp.maximum(variance, 1.0))
        for action in range(action_count):
            here = row == episode * action_count + action
            chosen = jnp.where(here, action_ref[episode, action], chosen)
            valid = mask_ref[episode, action].astype(jnp.float32)
            loss_weight = jnp.where(here, -valid * advantage / mask_total, loss_weight)
    shifted = logits - jnp.max(logits, axis=1, keepdims=True)
    log_all = shifted - jnp.log(jnp.sum(jnp.exp(shifted), axis=1, keepdims=True))
    picked = (lax.broadcasted_iota(jnp.int32, (rows, bins), 1) == chosen).astype(jnp.float32)
    logprob = jnp.sum(picked * log_all, axis=1, keepdims=True)
    logit_grad = (loss_weight * (picked - jnp.exp(log_all))).astype(jnp.bfloat16)
    pull_back = lax.dot_general(
        logit_grad, weight_ref[...], (((1,), (1,)), ((), ())), preferred_element_type=jnp.float32
    )
    for episode in range(episodes):
        mine = jnp.logical_and(row >= episode * action_count, row < (episode + 1) * action_count)
        pulls[episode : episode + 1, :] = jnp.sum(jnp.where(mine, pull_back, 0.0), axis=0, keepdims=True)
    grad_send[...] = logit_grad
    grad_all[group] = logit_grad

    block = 16 if chunk % 16 == 0 else 8

    def fill(target, slot, part, terms):
        at = pl.ds(part * span, span)
        scales = [pulls[episode : episode + 1, at] for episode in range(episodes)]

        def some(index, carry):
            here = pl.ds(pl.multiple_of(index * block, block), block)
            down = pl.ds(pl.multiple_of(slot * chunk + index * block, 8), block)
            total = moments[0, down, at] * scales[0]
            for episode in range(1, episodes):
                total = total + moments[episode, down, at] * scales[episode]
            for term in terms:
                total = total + term[here, :].astype(jnp.float32)
            target[here, :] = total.astype(jnp.bfloat16)
            return carry

        lax.fori_loop(0, chunk // block, some, 0)

    def hop(send, recv, sems, target, part, where):
        return remote(
            send.at[target, part],
            recv.at[target, part],
            sems.at[0, target, part],
            sems.at[1, target, part],
            where,
        )

    def pair_copy(target, part):
        return hop(pair_send, pair_recv, pair_sems, target, part, sibling)

    def up_copy(target, part):
        return hop(up_send, up_recv, up_sems, target, part, above)

    def down_copy(target, part):
        return hop(down_send, down_recv, down_sems, target, part, below)

    def give(target):
        for part in range(parts):
            fill(pair_send.at[target, part], 2 * target + 1 - core, part, [])
            pair_copy(target, part).start()

    last = n_out - 1
    for time in range(last):
        rising, falling = last + place - time, time - last + place

        @pl.when(time >= place)
        def _():
            give(rising)

        @pl.when(time >= last - place)
        def _():
            give(falling)

    give(place)

    for step, peer in enumerate(peers_g):
        to_all(grad_send, grad_all, grad_sems, step, group, (me, peer)).start()

    def pass_on(target, part, send, recv, copy):
        pair_copy(target, part).wait_recv()
        own = [pair_recv.at[target, part]]
        ends = place == 0 if copy is up_copy else place == last

        @pl.when(ends)
        def _():
            fill(send.at[target, part], 2 * target + core, part, own)

        @pl.when(jnp.logical_not(ends))
        def _():
            copy(target, part).wait_recv()
            fill(send.at[target, part], 2 * target + core, part, own + [recv.at[target, part]])

        copy(target, part).start()

    for time in range(last):
        rising, falling = last + place - time, time - last + place
        for part in range(parts):

            @pl.when(time >= place)
            def _():
                pass_on(rising, part, up_send, up_recv, up_copy)

            @pl.when(time >= last - place)
            def _():
                pass_on(falling, part, down_send, down_recv, down_copy)

    cell = lax.broadcasted_iota(jnp.int32, (episodes, action_count), 0) * action_count
    cell = cell + lax.broadcasted_iota(jnp.int32, (episodes, action_count), 1)
    laid = jnp.zeros((episodes, action_count), jnp.float32)
    for index in range(episodes * action_count):
        laid = jnp.where(cell == index, logprob[index : index + 1, :], laid)
    logprob_ref[...] = laid
    for peer in peers_g:
        to_all(head_ref, head_all, head_sems, 0, peer, (me, peer)).wait_recv()
        to_all(grad_send, grad_all, grad_sems, 0, peer, (me, peer)).wait_recv()
    grad_head_ref[...] = lax.dot_general(
        head_all[...].reshape(n_grp * rows, width),
        grad_all[...].reshape(n_grp * rows, bins),
        (((0,), (0,)), ((), ())),
        preferred_element_type=jnp.float32,
    ).astype(jnp.bfloat16)

    for part in range(parts):
        goal = out_ref.at[:, pl.ds(part * span, span)]
        pair_copy(place, part).wait_recv()
        own = [pair_recv.at[place, part]]
        rose, fell = up_recv.at[place, part], down_recv.at[place, part]

        @pl.when(place == 0)
        def _():
            down_copy(place, part).wait_recv()
            fill(goal, group, part, own + [fell])

        @pl.when(place == last)
        def _():
            up_copy(place, part).wait_recv()
            fill(goal, group, part, own + [rose])

        @pl.when(jnp.logical_and(place > 0, place < last))
        def _():
            up_copy(place, part).wait_recv()
            down_copy(place, part).wait_recv()
            fill(goal, group, part, own + [rose, fell])

    for target in range(n_out):
        for part in range(parts):
            pair_copy(target, part).wait_send()

            @pl.when(target > place)
            def _():
                up_copy(target, part).wait_send()

            @pl.when(target < place)
            def _():
                down_copy(target, part).wait_send()

    for step, peer in enumerate(peers):
        to_all(logits_send, logits_all, logits_sems, step, me, (peer, group)).wait_send()
    for step, peer in enumerate(peers_g):
        to_all(stats_send, stats_all, stats_sems, step, group, (me, peer)).wait_send()
        to_all(head_ref, head_all, head_sems, step, group, (me, peer)).wait_send()
        to_all(grad_send, grad_all, grad_sems, step, group, (me, peer)).wait_send()


def tail(actions, action_mask, group_ids, rewards, frames, slopes, head_input, head_weight):
    n_cp, n_grp = lax.axis_size("cp"), lax.axis_size("grp")
    n_out = n_grp // 2
    episodes = actions.shape[0]
    group_count = max(1, episodes * n_grp // 8)
    features, width = frames.shape[2], slopes.shape[2]
    rows, bins = head_input.shape[0], head_weight.shape[1]
    chunk, parts = features // n_grp, 2
    in_smem = pl.BlockSpec(memory_space=pltpu.SMEM)
    in_vmem = pl.BlockSpec(memory_space=pltpu.VMEM)
    dma = pltpu.SemaphoreType.DMA
    line = pltpu.VMEM((n_out, parts, chunk, width // parts), jnp.bfloat16)
    return pl.pallas_call(
        lambda *refs: tail_kernel(n_cp, n_out, group_count, *refs),
        out_shape=(
            jax.ShapeDtypeStruct(actions.shape, jnp.float32),
            jax.ShapeDtypeStruct((chunk, width), jnp.bfloat16),
            jax.ShapeDtypeStruct((width, bins), jnp.bfloat16),
        ),
        in_specs=[in_smem] * 4 + [in_vmem] * 4,
        out_specs=(in_vmem,) * 3,
        scratch_shapes=[
            pltpu.VMEM((rows, bins), jnp.float32),
            pltpu.VMEM((n_cp, rows, bins), jnp.float32),
            pltpu.VMEM((8, 128), jnp.float32),
            pltpu.VMEM((n_grp, 8, 128), jnp.float32),
            pltpu.VMEM((n_grp, rows, width), jnp.bfloat16),
            pltpu.VMEM((rows, bins), jnp.bfloat16),
            pltpu.VMEM((n_grp, rows, bins), jnp.bfloat16),
            pltpu.VMEM((-(-episodes // 8) * 8, width), jnp.float32),
            pltpu.VMEM((episodes, features, width), jnp.float32),
        ]
        + [line] * 6
        + [dma((2, n_cp))]
        + [dma((2, n_grp))] * 3
        + [dma((2, n_out, parts))] * 3,
        compiler_params=pltpu.CompilerParams(
            collective_id=1, has_side_effects=True, vmem_limit_bytes=60 * 1024 * 1024
        ),
        name="tail",
    )(actions, action_mask, group_ids, rewards, frames, slopes, head_input, head_weight)


def front_kernel(
    n_cp,
    n_out,
    length_ref,
    query_ref,
    key_ref,
    value_ref,
    map_ref,
    shard_ref,
    frames_ref,
    columns_ref,
    heads_all,
    blocks,
    map_held,
    total,
    local_sems,
    swap_send,
    swap_recv,
    block_send,
    block_recv,
    shard_send,
    shard_recv,
    pass_send,
    pass_recv,
):
    episodes, tokens, _ = query_ref.shape
    width = blocks.shape[2]
    seq = tokens * n_cp
    n_grp = 2 * n_out
    me, group = lax.axis_index("cp"), lax.axis_index("grp")
    place, core = group // 2, lax.rem(group, 2)
    sibling = 2 * place + 1 - core
    square = n_cp == 4
    if square:
        row_peer = me + 1 - 2 * lax.rem(me, 2)
        col_peer = lax.rem(me + 2, 4)
        far_peer = lax.rem(row_peer + 2, 4)
        peers = [far_peer, row_peer, col_peer]
    else:
        peers = [lax.rem(me + step, n_cp) for step in range(1, n_cp)]
    lines = [2 * lax.rem(place + step, n_out) + core for step in range(1, n_out)]

    map_copy = pltpu.make_async_copy(map_ref, map_held, local_sems.at[0])
    map_copy.start()
    keep_copy = pltpu.make_async_copy(shard_ref, columns_ref.at[group], local_sems.at[1])
    keep_copy.start()

    def my_copy(tensor, source, episode):
        return pltpu.make_async_copy(
            source.at[episode, :, pl.ds(pl.multiple_of(me * width, 128), width)],
            heads_all.at[tensor, episode, pl.ds(pl.multiple_of(me * tokens, 8), tokens), :],
            local_sems.at[2 + tensor * episodes + episode],
        )

    def swap_copy(tensor, source, episode, step, owner, peer):
        return remote(
            source.at[episode, :, pl.ds(pl.multiple_of(peer * width, 128), width)],
            heads_all.at[tensor, episode, pl.ds(pl.multiple_of(owner * tokens, 8), tokens), :],
            swap_send.at[tensor, episode, step],
            swap_recv.at[tensor, episode, owner],
            (peer, group),
        )

    sources = (query_ref, key_ref, value_ref)
    for episode in range(episodes):
        for tensor, source in enumerate(sources):
            my_copy(tensor, source, episode).start()
    greet([(peer, group) for peer in peers] + [(me, peer) for peer in lines] + [(me, sibling)])
    for episode in range(episodes):
        for tensor, source in enumerate(sources):
            for step, peer in enumerate(peers):
                swap_copy(tensor, source, episode, step, me, peer).start()

    def shard_copy(step, owner, peer):
        return remote(shard_ref, columns_ref.at[owner], shard_send.at[step], shard_recv.at[owner], (me, peer))

    def pass_copy(step, owner, source):
        return remote(source, columns_ref.at[owner], pass_send.at[step], pass_recv.at[owner], (me, sibling))

    for step, peer in reversed(list(enumerate(lines))):
        shard_copy(step, group, peer).start()
    pass_copy(n_out - 1, group, shard_ref).start()

    def rows_of(owner, episode, first, count):
        return blocks.at[owner, pl.ds(episode * seq + first, count), :]

    def block_copy(episode, step, owner, peer, first, count, part):
        return remote(
            rows_of(owner, episode, first, count),
            rows_of(owner, episode, first, count),
            block_send.at[episode, step],
            block_recv.at[episode, owner, part],
            (peer, group),
        )

    strip = min(seq, 256)

    def attend(episode):
        live = lax.broadcasted_iota(jnp.int32, (strip, seq), 1) < length_ref[episode]

        def one_head(head, carry):
            at = pl.ds(pl.multiple_of(head * HD, HD), HD)
            key_head = heads_all[1, episode, :, at]
            value_head = heads_all[2, episode, :, at]
            for first in range(0, seq, strip):
                query_head = heads_all[0, episode, first : first + strip, at]
                scores = lax.dot_general(
                    query_head, key_head, (((1,), (1,)), ((), ())), preferred_element_type=jnp.float32
                )
                scores = jnp.where(live, scores * (1.0 / math.sqrt(HD)), NEG_LARGE)
                probs = jnp.exp(scores - jnp.max(scores, axis=1, keepdims=True))
                row_total = jnp.sum(probs, axis=1, keepdims=True)
                weighted = jnp.dot(probs.astype(jnp.bfloat16), value_head, preferred_element_type=jnp.float32)
                blocks[me, episode * seq + first : episode * seq + first + strip, at] = (
                    weighted / row_total
                ).astype(jnp.bfloat16)
            return carry

        lax.fori_loop(0, width // HD, one_head, 0)

    def add_frames(episode, owner, opens, closes):
        tall = min(seq, 512)
        whole, spare = divmod(frames_ref.shape[2], 256)
        depth = pl.ds(pl.multiple_of(owner * width, 128), width)

        def one_tile(first, at):
            rows = pl.ds(episode * seq + first, tall)
            part = jnp.dot(blocks[owner, rows, :], map_held[depth, at], preferred_element_type=jnp.float32)
            if not opens:
                part = part + total[rows, at]
            if closes:
                frames_ref[episode, first : first + tall, at] = part.astype(jnp.bfloat16)
            else:
                total[rows, at] = part

        for first in range(0, seq, tall):

            def step(index, carry):
                one_tile(first, pl.ds(pl.multiple_of(index * 256, 256), 256))
                return carry

            lax.fori_loop(0, whole, step, 0)
            if spare:
                one_tile(first, pl.ds(whole * 256, spare))

    for episode in range(episodes):
        for tensor, source in enumerate(sources):
            my_copy(tensor, source, episode).wait()
            for peer in peers:
                swap_copy(tensor, source, episode, 0, peer, peer).wait_recv()
        attend(episode)
        if square:
            block_copy(episode, 0, me, row_peer, 0, seq, 0).start()
            block_copy(episode, 1, me, col_peer, 0, seq, 0).start()
        else:
            for step, peer in enumerate(peers):
                block_copy(episode, step, me, peer, 0, seq, 0).start()
        if episode == 0:
            map_copy.wait()
        add_frames(episode, me, True, False)

    def forward_shards():
        for step, peer in enumerate(lines):
            shard_copy(step, peer, peer).wait_recv()
            pass_copy(step, peer, columns_ref.at[peer]).start()

    half = seq // 2
    if square:
        for episode in range(episodes):
            block_copy(episode, 0, row_peer, row_peer, 0, seq, 0).wait_recv()
            block_copy(episode, 2, row_peer, col_peer, 0, half, 0).start()
            block_copy(episode, 1, col_peer, col_peer, 0, seq, 0).wait_recv()
            block_copy(episode, 3, col_peer, row_peer, half, half, 1).start()
            add_frames(episode, row_peer, False, False)
            add_frames(episode, col_peer, False, False)
        forward_shards()
        for episode in range(episodes):
            block_copy(episode, 2, far_peer, col_peer, 0, half, 0).wait_recv()
            block_copy(episode, 3, far_peer, row_peer, half, half, 1).wait_recv()
            add_frames(episode, far_peer, False, True)
    else:
        for episode in range(episodes):
            for step, peer in enumerate(peers):
                block_copy(episode, step, peer, peer, 0, seq, 0).wait_recv()
                add_frames(episode, peer, False, step == len(peers) - 1)
        forward_shards()

    for step, peer in enumerate(lines):
        pass_copy(step, peer + 1 - 2 * core, columns_ref.at[peer]).wait_recv()
    pass_copy(n_out - 1, sibling, shard_ref).wait_recv()
    keep_copy.wait()
    for episode in range(episodes):
        for tensor, source in enumerate(sources):
            for step, peer in enumerate(peers):
                swap_copy(tensor, source, episode, step, me, peer).wait_send()
        if square:
            block_copy(episode, 0, me, row_peer, 0, seq, 0).wait_send()
            block_copy(episode, 1, me, col_peer, 0, seq, 0).wait_send()
            block_copy(episode, 2, row_peer, col_peer, 0, half, 0).wait_send()
            block_copy(episode, 3, col_peer, row_peer, half, half, 1).wait_send()
        else:
            for step, peer in enumerate(peers):
                block_copy(episode, step, me, peer, 0, seq, 0).wait_send()
    for step, peer in enumerate(lines):
        shard_copy(step, group, peer).wait_send()
        pass_copy(step, peer, columns_ref.at[peer]).wait_send()
    pass_copy(n_out - 1, group, shard_ref).wait_send()


def front(queries, keys, values, lengths, frame_map, proj_weight):
    n_cp, n_grp = lax.axis_size("cp"), lax.axis_size("grp")
    n_out = n_grp // 2
    episodes, tokens, att_width = queries.shape
    seq, width = tokens * n_cp, att_width // n_cp
    chunk, cols = proj_weight.shape
    features = frame_map.shape[1]
    anywhere = pl.BlockSpec(memory_space=pl.ANY)
    in_vmem = pl.BlockSpec(memory_space=pltpu.VMEM)
    dma = pltpu.SemaphoreType.DMA
    frames, columns = pl.pallas_call(
        lambda *refs: front_kernel(n_cp, n_out, *refs),
        out_shape=(
            jax.ShapeDtypeStruct((episodes, seq, features), jnp.bfloat16),
            jax.ShapeDtypeStruct((n_grp, chunk, cols), jnp.bfloat16),
        ),
        in_specs=[pl.BlockSpec(memory_space=pltpu.SMEM)] + [anywhere] * 4 + [in_vmem],
        out_specs=(in_vmem, anywhere),
        scratch_shapes=[
            pltpu.VMEM((3, episodes, seq, width), jnp.bfloat16),
            pltpu.VMEM((n_cp, episodes * seq, width), jnp.bfloat16),
            pltpu.VMEM(frame_map.shape, jnp.bfloat16),
            pltpu.VMEM((episodes * seq, features), jnp.float32),
            dma((2 + 3 * episodes,)),
            dma((3, episodes, n_cp)),
            dma((3, episodes, n_cp)),
            dma((episodes, max(n_cp, 4))),
            dma((episodes, n_cp, 2)),
            dma((n_out,)),
            dma((n_grp,)),
            dma((n_out,)),
            dma((n_grp,)),
        ],
        compiler_params=pltpu.CompilerParams(
            collective_id=3, has_side_effects=True, vmem_limit_bytes=60 * 1024 * 1024
        ),
        name="front",
    )(lengths, queries, keys, values, frame_map, proj_weight)
    return frames, columns.reshape(n_grp * chunk, cols)


def per_device(
    queries,
    keys,
    values,
    lengths,
    frame_map,
    proj_weight,
    head_weight,
    act_embed,
    actions,
    action_mask,
    group_ids,
    rewards,
):
    episodes_here, tokens_here, att_width = queries.shape
    action_count = act_embed.shape[0]
    lengths_real = lengths.astype(jnp.float32)
    all_frames, proj_cols = front(queries, keys, values, lengths, frame_map, proj_weight)
    seq_span = all_frames.shape[1]
    flat_frames = all_frames.reshape(episodes_here * seq_span, all_frames.shape[2])
    col_count = proj_cols.shape[1]
    pre_act = jnp.dot(flat_frames, proj_cols, preferred_element_type=jnp.float32).reshape(
        episodes_here, seq_span, col_count
    )
    hidden = gelu_exact(pre_act)
    token_mask = (jnp.arange(seq_span, dtype=jnp.int32)[None, :] < lengths[:, None]).astype(
        jnp.float32
    )
    pooled = jnp.sum(token_mask[:, :, None] * hidden, axis=1) / lengths_real[:, None]
    sum_input = pooled[:, None, :] + act_embed[None, :, :]
    head_input = sum_input.astype(jnp.bfloat16).reshape(episodes_here * action_count, col_count)
    spare = -head_input.shape[0] % 16
    scaled_mask = token_mask / lengths_real[:, None]
    slopes = (scaled_mask[:, :, None] * gelu_slope(pre_act)).astype(jnp.bfloat16)
    logprobs, grad_proj, grad_head = tail(
        actions,
        action_mask,
        group_ids,
        rewards,
        all_frames,
        slopes,
        jnp.pad(head_input, ((0, spare), (0, 0))),
        head_weight,
    )
    return (logprobs, grad_proj, grad_head)


def solution(mesh):
    in_specs = (
        P("grp", "cp", None),
        P("grp", "cp", None),
        P("grp", "cp", None),
        P("grp"),
        P(),
        P("grp", "cp"),
        P("cp", None),
        P(None, "cp"),
        P("grp", None),
        P("grp", None),
        P("grp"),
        P("grp"),
    )
    out_specs = (P("grp", None), P("grp", "cp"), P("cp", None))
    return jax.shard_map(
        per_device, mesh=mesh, in_specs=in_specs, out_specs=out_specs, check_vma=False
    )
```

```python
import math

import jax
import jax.numpy as jnp
from jax import lax
from jax.experimental import pallas as pl
from jax.experimental.pallas import tpu as pltpu
from jax.sharding import PartitionSpec as P

HD = 128
ON_MESH = pl.DeviceIdType.MESH

SQRT_HALF = 0.7071067811865476
INV_ROOT_TAU = 0.3989422804014327
NEG_LARGE = -1e30


def gelu_exact(values_in):
    return 0.5 * values_in * (1.0 + lax.erf(values_in * SQRT_HALF))


def gelu_slope(values_in):
    return (
        0.5 * (1.0 + lax.erf(values_in * SQRT_HALF))
        + values_in * jnp.exp(-0.5 * values_in * values_in) * INV_ROOT_TAU
    )


def remote(source, target, send_sem, recv_sem, where):
    return pltpu.make_async_remote_copy(
        src_ref=source,
        dst_ref=target,
        send_sem=send_sem,
        recv_sem=recv_sem,
        device_id=where,
        device_id_type=ON_MESH,
    )


def greet(peers):
    barrier = pltpu.get_barrier_semaphore()
    for where in peers:
        pl.semaphore_signal(barrier, inc=1, device_id=where, device_id_type=ON_MESH)
    pl.semaphore_wait(barrier, len(peers))


def tail_kernel(
    n_cp,
    n_out,
    group_count,
    action_ref,
    mask_ref,
    id_ref,
    reward_ref,
    frames_ref,
    slope_ref,
    pooled_ref,
    embed_ref,
    weight_ref,
    logprob_ref,
    out_ref,
    grad_head_ref,
    head_rows,
    head_ref,
    logits_send,
    logits_all,
    stats_send,
    stats_all,
    head_all,
    grad_send,
    grad_all,
    pulls,
    moments,
    pair_send,
    pair_recv,
    up_send,
    up_recv,
    down_send,
    down_recv,
    logits_sems,
    stats_sems,
    head_sems,
    grad_sems,
    pair_sems,
    up_sems,
    down_sems,
):
    episodes, action_count = action_ref.shape
    rows, _ = head_ref.shape
    bins = weight_ref.shape[1]
    seq = frames_ref.shape[1]
    chunk, width = out_ref.shape
    parts, span = pair_send.shape[1], pair_send.shape[3]
    n_grp = 2 * n_out
    me, group = lax.axis_index("cp"), lax.axis_index("grp")
    place, core = group // 2, lax.rem(group, 2)
    sibling = (me, 2 * place + 1 - core)
    above, below = (me, lax.rem(group + 2, n_grp)), (me, lax.rem(group + n_grp - 2, n_grp))
    peers = [lax.rem(me + step, n_cp) for step in range(1, n_cp)]
    peers_g = [lax.rem(group + step, n_grp) for step in range(1, n_grp)]

    def to_all(send, everyone, sems, step, owner, where):
        return remote(send, everyone.at[owner], sems.at[0, step], sems.at[1, owner], where)

    lane = lax.broadcasted_iota(jnp.int32, (8, 128), 1)
    stats = jnp.zeros((8, 128), jnp.float32)
    for episode in range(episodes):
        reward, member = reward_ref[episode], id_ref[episode]
        stats = stats + jnp.where(lane == member, reward, 0.0)
        stats = stats + jnp.where(lane == group_count + member, reward * reward, 0.0)
        stats = stats + jnp.where(lane == 2 * group_count + member, 1.0, 0.0)
        for action in range(action_count):
            valid = mask_ref[episode, action].astype(jnp.float32)
            stats = stats + jnp.where(lane == 3 * group_count, valid, 0.0)
    stats_send[...] = stats
    stats_all[group] = stats
    head_rows[...] = jnp.zeros_like(head_rows)
    for episode in range(episodes):
        head_rows[episode * action_count : (episode + 1) * action_count, :] = (
            pooled_ref[episode : episode + 1, :] + embed_ref[...]
        )
    head_ref[...] = head_rows[...].astype(jnp.bfloat16)
    partial = jnp.dot(head_ref[...], weight_ref[...], preferred_element_type=jnp.float32)
    logits_send[...] = partial
    logits_all[me] = partial
    head_all[group] = head_ref[...]

    greet([(peer, group) for peer in peers] + [(me, peer) for peer in peers_g])
    for step, peer in enumerate(peers):
        to_all(logits_send, logits_all, logits_sems, step, me, (peer, group)).start()
    for step, peer in enumerate(peers_g):
        to_all(stats_send, stats_all, stats_sems, step, group, (me, peer)).start()
    for step, peer in enumerate(peers_g):
        to_all(head_ref, head_all, head_sems, step, group, (me, peer)).start()

    features = frames_ref.shape[2]
    whole, spare = divmod(features, 256)

    def moment(episode, at, down):
        moments[episode, down, :] = lax.dot_general(
            frames_ref[episode, :, at],
            slope_ref[episode],
            (((0,), (0,)), ((), ())),
            preferred_element_type=jnp.float32,
        )

    for episode in range(episodes):

        def one_tile(index, carry):
            at = pl.ds(pl.multiple_of(index * 256, 256), 256)
            moment(episode, at, at)
            return carry

        lax.fori_loop(0, whole, one_tile, 0)
        if spare:
            moment(episode, pl.ds(whole * 256, spare), pl.ds(whole * 256, spare))

    for peer in peers:
        to_all(logits_send, logits_all, logits_sems, 0, peer, (peer, group)).wait_recv()
    logits = logits_all[0]
    for slot in range(1, n_cp):
        logits = logits + logits_all[slot]
    for peer in peers_g:
        to_all(stats_send, stats_all, stats_sems, 0, peer, (me, peer)).wait_recv()
    stats = jnp.sum(stats_all[...], axis=0)[0:1]
    lane = lane[0:1]

    def entry(index):
        return jnp.sum(jnp.where(lane == index, stats, 0.0), axis=1, keepdims=True)

    mask_total = jnp.maximum(entry(3 * group_count), 1.0)
    row = lax.broadcasted_iota(jnp.int32, (rows, 1), 0)
    chosen = jnp.zeros((rows, 1), jnp.int32)
    loss_weight = jnp.zeros((rows, 1), jnp.float32)
    for episode in range(episodes):
        member = id_ref[episode]
        size = jnp.maximum(entry(2 * group_count + member), 1.0)
        mean = entry(member) / size
        variance = entry(group_count + member) / size - mean * mean
        advantage = (reward_ref[episode] - mean) / jnp.sqrt(jnp.maximum(variance, 1.0))
        for action in range(action_count):
            here = row == episode * action_count + action
            chosen = jnp.where(here, action_ref[episode, action], chosen)
            valid = mask_ref[episode, action].astype(jnp.float32)
            loss_weight = jnp.where(here, -valid * advantage / mask_total, loss_weight)
    shifted = logits - jnp.max(logits, axis=1, keepdims=True)
    log_all = shifted - jnp.log(jnp.sum(jnp.exp(shifted), axis=1, keepdims=True))
    picked = (lax.broadcasted_iota(jnp.int32, (rows, bins), 1) == chosen).astype(jnp.float32)
    logprob = jnp.sum(picked * log_all, axis=1, keepdims=True)
    logit_grad = (loss_weight * (picked - jnp.exp(log_all))).astype(jnp.bfloat16)
    pull_back = lax.dot_general(
        logit_grad, weight_ref[...], (((1,), (1,)), ((), ())), preferred_element_type=jnp.float32
    )
    for episode in range(episodes):
        mine = jnp.logical_and(row >= episode * action_count, row < (episode + 1) * action_count)
        pulls[episode : episode + 1, :] = jnp.sum(jnp.where(mine, pull_back, 0.0), axis=0, keepdims=True)
    grad_send[...] = logit_grad
    grad_all[group] = logit_grad

    block = 16 if chunk % 16 == 0 else 8

    def fill(target, slot, part, terms):
        at = pl.ds(part * span, span)
        scales = [pulls[episode : episode + 1, at] for episode in range(episodes)]

        def some(index, carry):
            here = pl.ds(pl.multiple_of(index * block, block), block)
            down = pl.ds(pl.multiple_of(slot * chunk + index * block, 8), block)
            total = moments[0, down, at] * scales[0]
            for episode in range(1, episodes):
                total = total + moments[episode, down, at] * scales[episode]
            for term in terms:
                total = total + term[here, :].astype(jnp.float32)
            target[here, :] = total.astype(jnp.bfloat16)
            return carry

        lax.fori_loop(0, chunk // block, some, 0)

    def hop(send, recv, sems, target, part, where):
        return remote(
            send.at[target, part],
            recv.at[target, part],
            sems.at[0, target, part],
            sems.at[1, target, part],
            where,
        )

    def pair_copy(target, part):
        return hop(pair_send, pair_recv, pair_sems, target, part, sibling)

    def up_copy(target, part):
        return hop(up_send, up_recv, up_sems, target, part, above)

    def down_copy(target, part):
        return hop(down_send, down_recv, down_sems, target, part, below)

    def give(target):
        for part in range(parts):
            fill(pair_send.at[target, part], 2 * target + 1 - core, part, [])
            pair_copy(target, part).start()

    last = n_out - 1
    for time in range(last):
        rising, falling = last + place - time, time - last + place

        @pl.when(time >= place)
        def _():
            give(rising)

        @pl.when(time >= last - place)
        def _():
            give(falling)

    give(place)

    for step, peer in enumerate(peers_g):
        to_all(grad_send, grad_all, grad_sems, step, group, (me, peer)).start()

    def pass_on(target, part, send, recv, copy):
        pair_copy(target, part).wait_recv()
        own = [pair_recv.at[target, part]]
        ends = place == 0 if copy is up_copy else place == last

        @pl.when(ends)
        def _():
            fill(send.at[target, part], 2 * target + core, part, own)

        @pl.when(jnp.logical_not(ends))
        def _():
            copy(target, part).wait_recv()
            fill(send.at[target, part], 2 * target + core, part, own + [recv.at[target, part]])

        copy(target, part).start()

    for time in range(last):
        rising, falling = last + place - time, time - last + place
        for part in range(parts):

            @pl.when(time >= place)
            def _():
                pass_on(rising, part, up_send, up_recv, up_copy)

            @pl.when(time >= last - place)
            def _():
                pass_on(falling, part, down_send, down_recv, down_copy)

    cell = lax.broadcasted_iota(jnp.int32, (episodes, action_count), 0) * action_count
    cell = cell + lax.broadcasted_iota(jnp.int32, (episodes, action_count), 1)
    laid = jnp.zeros((episodes, action_count), jnp.float32)
    for index in range(episodes * action_count):
        laid = jnp.where(cell == index, logprob[index : index + 1, :], laid)
    logprob_ref[...] = laid
    for peer in peers_g:
        to_all(head_ref, head_all, head_sems, 0, peer, (me, peer)).wait_recv()
        to_all(grad_send, grad_all, grad_sems, 0, peer, (me, peer)).wait_recv()
    grad_head_ref[...] = lax.dot_general(
        head_all[...].reshape(n_grp * rows, width),
        grad_all[...].reshape(n_grp * rows, bins),
        (((0,), (0,)), ((), ())),
        preferred_element_type=jnp.float32,
    ).astype(jnp.bfloat16)

    for part in range(parts):
        goal = out_ref.at[:, pl.ds(part * span, span)]
        pair_copy(place, part).wait_recv()
        own = [pair_recv.at[place, part]]
        rose, fell = up_recv.at[place, part], down_recv.at[place, part]

        @pl.when(place == 0)
        def _():
            down_copy(place, part).wait_recv()
            fill(goal, group, part, own + [fell])

        @pl.when(place == last)
        def _():
            up_copy(place, part).wait_recv()
            fill(goal, group, part, own + [rose])

        @pl.when(jnp.logical_and(place > 0, place < last))
        def _():
            up_copy(place, part).wait_recv()
            down_copy(place, part).wait_recv()
            fill(goal, group, part, own + [rose, fell])

    for target in range(n_out):
        for part in range(parts):
            pair_copy(target, part).wait_send()

            @pl.when(target > place)
            def _():
                up_copy(target, part).wait_send()

            @pl.when(target < place)
            def _():
                down_copy(target, part).wait_send()

    for step, peer in enumerate(peers):
        to_all(logits_send, logits_all, logits_sems, step, me, (peer, group)).wait_send()
    for step, peer in enumerate(peers_g):
        to_all(stats_send, stats_all, stats_sems, step, group, (me, peer)).wait_send()
        to_all(head_ref, head_all, head_sems, step, group, (me, peer)).wait_send()
        to_all(grad_send, grad_all, grad_sems, step, group, (me, peer)).wait_send()


def tail(actions, action_mask, group_ids, rewards, frames, slopes, pooled, act_embed, head_weight):
    n_cp, n_grp = lax.axis_size("cp"), lax.axis_size("grp")
    n_out = n_grp // 2
    episodes = actions.shape[0]
    group_count = max(1, episodes * n_grp // 8)
    features, width = frames.shape[2], slopes.shape[2]
    rows, bins = -(-actions.size // 16) * 16, head_weight.shape[1]
    chunk, parts = features // n_grp, 2
    in_smem = pl.BlockSpec(memory_space=pltpu.SMEM)
    in_vmem = pl.BlockSpec(memory_space=pltpu.VMEM)
    dma = pltpu.SemaphoreType.DMA
    line = pltpu.VMEM((n_out, parts, chunk, width // parts), jnp.bfloat16)
    return pl.pallas_call(
        lambda *refs: tail_kernel(n_cp, n_out, group_count, *refs),
        out_shape=(
            jax.ShapeDtypeStruct(actions.shape, jnp.float32),
            jax.ShapeDtypeStruct((chunk, width), jnp.bfloat16),
            jax.ShapeDtypeStruct((width, bins), jnp.bfloat16),
        ),
        in_specs=[in_smem] * 4 + [in_vmem] * 5,
        out_specs=(in_vmem,) * 3,
        scratch_shapes=[
            pltpu.VMEM((rows, width), jnp.float32),
            pltpu.VMEM((rows, width), jnp.bfloat16),
            pltpu.VMEM((rows, bins), jnp.float32),
            pltpu.VMEM((n_cp, rows, bins), jnp.float32),
            pltpu.VMEM((8, 128), jnp.float32),
            pltpu.VMEM((n_grp, 8, 128), jnp.float32),
            pltpu.VMEM((n_grp, rows, width), jnp.bfloat16),
            pltpu.VMEM((rows, bins), jnp.bfloat16),
            pltpu.VMEM((n_grp, rows, bins), jnp.bfloat16),
            pltpu.VMEM((-(-episodes // 8) * 8, width), jnp.float32),
            pltpu.VMEM((episodes, features, width), jnp.float32),
        ]
        + [line] * 6
        + [dma((2, n_cp))]
        + [dma((2, n_grp))] * 3
        + [dma((2, n_out, parts))] * 3,
        compiler_params=pltpu.CompilerParams(
            collective_id=1, has_side_effects=True, vmem_limit_bytes=60 * 1024 * 1024
        ),
        name="tail",
    )(actions, action_mask, group_ids, rewards, frames, slopes, pooled, act_embed, head_weight)


def front_kernel(
    n_cp,
    n_out,
    length_ref,
    query_ref,
    key_ref,
    value_ref,
    map_ref,
    shard_ref,
    frames_ref,
    columns_ref,
    scale_ref,
    heads_all,
    blocks,
    map_held,
    total,
    local_sems,
    swap_send,
    swap_recv,
    block_send,
    block_recv,
    shard_send,
    shard_recv,
    pass_send,
    pass_recv,
):
    episodes, tokens, _ = query_ref.shape
    width = blocks.shape[2]
    seq = tokens * n_cp
    n_grp = 2 * n_out
    me, group = lax.axis_index("cp"), lax.axis_index("grp")
    place, core = group // 2, lax.rem(group, 2)
    sibling = 2 * place + 1 - core
    square = n_cp == 4
    if square:
        row_peer = me + 1 - 2 * lax.rem(me, 2)
        col_peer = lax.rem(me + 2, 4)
        far_peer = lax.rem(row_peer + 2, 4)
        peers = [far_peer, row_peer, col_peer]
    else:
        peers = [lax.rem(me + step, n_cp) for step in range(1, n_cp)]
    lines = [2 * lax.rem(place + step, n_out) + core for step in range(1, n_out)]

    map_copy = pltpu.make_async_copy(map_ref, map_held, local_sems.at[0])
    map_copy.start()
    keep_copy = pltpu.make_async_copy(shard_ref, columns_ref.at[group], local_sems.at[1])
    keep_copy.start()

    def my_copy(tensor, source, episode):
        return pltpu.make_async_copy(
            source.at[episode, :, pl.ds(pl.multiple_of(me * width, 128), width)],
            heads_all.at[tensor, episode, pl.ds(pl.multiple_of(me * tokens, 8), tokens), :],
            local_sems.at[2 + tensor * episodes + episode],
        )

    def swap_copy(tensor, source, episode, step, owner, peer):
        return remote(
            source.at[episode, :, pl.ds(pl.multiple_of(peer * width, 128), width)],
            heads_all.at[tensor, episode, pl.ds(pl.multiple_of(owner * tokens, 8), tokens), :],
            swap_send.at[tensor, episode, step],
            swap_recv.at[tensor, episode, owner],
            (peer, group),
        )

    sources = (query_ref, key_ref, value_ref)
    for episode in range(episodes):
        for tensor, source in enumerate(sources):
            my_copy(tensor, source, episode).start()
    greet([(peer, group) for peer in peers] + [(me, peer) for peer in lines] + [(me, sibling)])
    for episode in range(episodes):
        for tensor, source in enumerate(sources):
            for step, peer in enumerate(peers):
                swap_copy(tensor, source, episode, step, me, peer).start()

    def shard_copy(step, owner, peer):
        return remote(shard_ref, columns_ref.at[owner], shard_send.at[step], shard_recv.at[owner], (me, peer))

    def pass_copy(step, owner, source):
        return remote(source, columns_ref.at[owner], pass_send.at[step], pass_recv.at[owner], (me, sibling))

    for step, peer in reversed(list(enumerate(lines))):
        shard_copy(step, group, peer).start()
    pass_copy(n_out - 1, group, shard_ref).start()

    def rows_of(owner, episode, first, count):
        return blocks.at[owner, pl.ds(episode * seq + first, count), :]

    def block_copy(episode, step, owner, peer, first, count, part):
        return remote(
            rows_of(owner, episode, first, count),
            rows_of(owner, episode, first, count),
            block_send.at[episode, step],
            block_recv.at[episode, owner, part],
            (peer, group),
        )

    for episode in range(episodes):
        length = jnp.full((1, seq), length_ref[episode], jnp.int32)
        kept = lax.broadcasted_iota(jnp.int32, (1, seq), 1) < length
        scale_ref[episode : episode + 1, :] = jnp.where(kept, 1.0 / length.astype(jnp.float32), 0.0)

    strip = min(seq, 256)

    def attend(episode):
        live = lax.broadcasted_iota(jnp.int32, (strip, seq), 1) < length_ref[episode]

        def one_head(head, carry):
            at = pl.ds(pl.multiple_of(head * HD, HD), HD)
            key_head = heads_all[1, episode, :, at]
            value_head = heads_all[2, episode, :, at]
            for first in range(0, seq, strip):
                query_head = heads_all[0, episode, first : first + strip, at]
                scores = lax.dot_general(
                    query_head, key_head, (((1,), (1,)), ((), ())), preferred_element_type=jnp.float32
                )
                scores = jnp.where(live, scores * (1.0 / math.sqrt(HD)), NEG_LARGE)
                probs = jnp.exp(scores - jnp.max(scores, axis=1, keepdims=True))
                row_total = jnp.sum(probs, axis=1, keepdims=True)
                weighted = jnp.dot(probs.astype(jnp.bfloat16), value_head, preferred_element_type=jnp.float32)
                blocks[me, episode * seq + first : episode * seq + first + strip, at] = (
                    weighted / row_total
                ).astype(jnp.bfloat16)
            return carry

        lax.fori_loop(0, width // HD, one_head, 0)

    def add_frames(episode, owner, opens, closes):
        tall = min(seq, 512)
        whole, spare = divmod(frames_ref.shape[2], 256)
        depth = pl.ds(pl.multiple_of(owner * width, 128), width)

        def one_tile(first, at):
            rows = pl.ds(episode * seq + first, tall)
            part = jnp.dot(blocks[owner, rows, :], map_held[depth, at], preferred_element_type=jnp.float32)
            if not opens:
                part = part + total[rows, at]
            if closes:
                frames_ref[episode, first : first + tall, at] = part.astype(jnp.bfloat16)
            else:
                total[rows, at] = part

        for first in range(0, seq, tall):

            def step(index, carry):
                one_tile(first, pl.ds(pl.multiple_of(index * 256, 256), 256))
                return carry

            lax.fori_loop(0, whole, step, 0)
            if spare:
                one_tile(first, pl.ds(whole * 256, spare))

    for episode in range(episodes):
        for tensor, source in enumerate(sources):
            my_copy(tensor, source, episode).wait()
            for peer in peers:
                swap_copy(tensor, source, episode, 0, peer, peer).wait_recv()
        attend(episode)
        if square:
            block_copy(episode, 0, me, row_peer, 0, seq, 0).start()
            block_copy(episode, 1, me, col_peer, 0, seq, 0).start()
        else:
            for step, peer in enumerate(peers):
                block_copy(episode, step, me, peer, 0, seq, 0).start()
        if episode == 0:
            map_copy.wait()
        add_frames(episode, me, True, False)

    def forward_shards():
        for step, peer in enumerate(lines):
            shard_copy(step, peer, peer).wait_recv()
            pass_copy(step, peer, columns_ref.at[peer]).start()

    half = seq // 2
    if square:
        for episode in range(episodes):
            block_copy(episode, 0, row_peer, row_peer, 0, seq, 0).wait_recv()
            block_copy(episode, 2, row_peer, col_peer, 0, half, 0).start()
            block_copy(episode, 1, col_peer, col_peer, 0, seq, 0).wait_recv()
            block_copy(episode, 3, col_peer, row_peer, half, half, 1).start()
            if episode == 0:
                forward_shards()
            add_frames(episode, row_peer, False, False)
            add_frames(episode, col_peer, False, False)
        for episode in range(episodes):
            block_copy(episode, 2, far_peer, col_peer, 0, half, 0).wait_recv()
            block_copy(episode, 3, far_peer, row_peer, half, half, 1).wait_recv()
            add_frames(episode, far_peer, False, True)
    else:
        for episode in range(episodes):
            for step, peer in enumerate(peers):
                block_copy(episode, step, peer, peer, 0, seq, 0).wait_recv()
                add_frames(episode, peer, False, step == len(peers) - 1)
        forward_shards()

    for step, peer in enumerate(lines):
        pass_copy(step, peer + 1 - 2 * core, columns_ref.at[peer]).wait_recv()
    pass_copy(n_out - 1, sibling, shard_ref).wait_recv()
    keep_copy.wait()
    for episode in range(episodes):
        for tensor, source in enumerate(sources):
            for step, peer in enumerate(peers):
                swap_copy(tensor, source, episode, step, me, peer).wait_send()
        if square:
            block_copy(episode, 0, me, row_peer, 0, seq, 0).wait_send()
            block_copy(episode, 1, me, col_peer, 0, seq, 0).wait_send()
            block_copy(episode, 2, row_peer, col_peer, 0, half, 0).wait_send()
            block_copy(episode, 3, col_peer, row_peer, half, half, 1).wait_send()
        else:
            for step, peer in enumerate(peers):
                block_copy(episode, step, me, peer, 0, seq, 0).wait_send()
    for step, peer in enumerate(lines):
        shard_copy(step, group, peer).wait_send()
        pass_copy(step, peer, columns_ref.at[peer]).wait_send()
    pass_copy(n_out - 1, group, shard_ref).wait_send()


def front(queries, keys, values, lengths, frame_map, proj_weight):
    n_cp, n_grp = lax.axis_size("cp"), lax.axis_size("grp")
    n_out = n_grp // 2
    episodes, tokens, att_width = queries.shape
    seq, width = tokens * n_cp, att_width // n_cp
    chunk, cols = proj_weight.shape
    features = frame_map.shape[1]
    anywhere = pl.BlockSpec(memory_space=pl.ANY)
    in_vmem = pl.BlockSpec(memory_space=pltpu.VMEM)
    dma = pltpu.SemaphoreType.DMA
    frames, columns, token_scale = pl.pallas_call(
        lambda *refs: front_kernel(n_cp, n_out, *refs),
        out_shape=(
            jax.ShapeDtypeStruct((episodes, seq, features), jnp.bfloat16),
            jax.ShapeDtypeStruct((n_grp, chunk, cols), jnp.bfloat16),
            jax.ShapeDtypeStruct((episodes, seq), jnp.float32),
        ),
        in_specs=[pl.BlockSpec(memory_space=pltpu.SMEM)] + [anywhere] * 4 + [in_vmem],
        out_specs=(in_vmem, anywhere, in_vmem),
        scratch_shapes=[
            pltpu.VMEM((3, episodes, seq, width), jnp.bfloat16),
            pltpu.VMEM((n_cp, episodes * seq, width), jnp.bfloat16),
            pltpu.VMEM(frame_map.shape, jnp.bfloat16),
            pltpu.VMEM((episodes * seq, features), jnp.float32),
            dma((2 + 3 * episodes,)),
            dma((3, episodes, n_cp)),
            dma((3, episodes, n_cp)),
            dma((episodes, max(n_cp, 4))),
            dma((episodes, n_cp, 2)),
            dma((n_out,)),
            dma((n_grp,)),
            dma((n_out,)),
            dma((n_grp,)),
        ],
        compiler_params=pltpu.CompilerParams(
            collective_id=3, has_side_effects=True, vmem_limit_bytes=60 * 1024 * 1024
        ),
        name="front",
    )(lengths, queries, keys, values, frame_map, proj_weight)
    return frames, columns.reshape(n_grp * chunk, cols), token_scale


def write_kernel(first, second, third, first_out, second_out, third_out):
    first_out[...] = first[...]
    second_out[...] = second[...]
    third_out[...] = third[...]


def write_out(*results):
    in_vmem = pl.BlockSpec(memory_space=pltpu.VMEM)
    return pl.pallas_call(
        write_kernel,
        out_shape=tuple(jax.ShapeDtypeStruct(result.shape, result.dtype) for result in results),
        in_specs=[in_vmem] * 3,
        out_specs=(in_vmem,) * 3,
        name="write_out",
    )(*results)


def per_device(
    queries,
    keys,
    values,
    lengths,
    frame_map,
    proj_weight,
    head_weight,
    act_embed,
    actions,
    action_mask,
    group_ids,
    rewards,
):
    episodes_here, tokens_here, att_width = queries.shape
    all_frames, proj_cols, token_scale = front(queries, keys, values, lengths, frame_map, proj_weight)
    seq_span = all_frames.shape[1]
    flat_frames = all_frames.reshape(episodes_here * seq_span, all_frames.shape[2])
    col_count = proj_cols.shape[1]
    pre_act = jnp.dot(flat_frames, proj_cols, preferred_element_type=jnp.float32).reshape(
        episodes_here, seq_span, col_count
    )
    hidden = gelu_exact(pre_act)
    pooled = jnp.sum(token_scale[:, :, None] * hidden, axis=1)
    slopes = (token_scale[:, :, None] * gelu_slope(pre_act)).astype(jnp.bfloat16)
    logprobs, grad_proj, grad_head = tail(
        actions,
        action_mask,
        group_ids,
        rewards,
        all_frames,
        slopes,
        pooled,
        act_embed,
        head_weight,
    )
    return write_out(logprobs, grad_proj, grad_head)


def solution(mesh):
    in_specs = (
        P("grp", "cp", None),
        P("grp", "cp", None),
        P("grp", "cp", None),
        P("grp"),
        P(),
        P("grp", "cp"),
        P("cp", None),
        P(None, "cp"),
        P("grp", None),
        P("grp", None),
        P("grp"),
        P("grp"),
    )
    out_specs = (P("grp", None), P("grp", "cp"), P("cp", None))
    return jax.shard_map(
        per_device, mesh=mesh, in_specs=in_specs, out_specs=out_specs, check_vma=False
    )
```

```python
import math

import jax
import jax.numpy as jnp
from jax import lax
from jax.experimental import pallas as pl
from jax.experimental.pallas import tpu as pltpu
from jax.sharding import PartitionSpec as P

HD = 128
ON_MESH = pl.DeviceIdType.MESH

SQRT_HALF = 0.7071067811865476
INV_ROOT_TAU = 0.3989422804014327
NEG_LARGE = -1e30


def gelu_exact(values_in):
    return 0.5 * values_in * (1.0 + lax.erf(values_in * SQRT_HALF))


def gelu_slope(values_in):
    return (
        0.5 * (1.0 + lax.erf(values_in * SQRT_HALF))
        + values_in * jnp.exp(-0.5 * values_in * values_in) * INV_ROOT_TAU
    )


def remote(source, target, send_sem, recv_sem, where):
    return pltpu.make_async_remote_copy(
        src_ref=source,
        dst_ref=target,
        send_sem=send_sem,
        recv_sem=recv_sem,
        device_id=where,
        device_id_type=ON_MESH,
    )


def greet(peers):
    barrier = pltpu.get_barrier_semaphore()
    for where in peers:
        pl.semaphore_signal(barrier, inc=1, device_id=where, device_id_type=ON_MESH)
    pl.semaphore_wait(barrier, len(peers))


def tail_kernel(
    n_cp,
    n_out,
    group_count,
    action_ref,
    mask_ref,
    id_ref,
    reward_ref,
    frames_ref,
    slope_ref,
    pooled_ref,
    embed_ref,
    weight_ref,
    logprob_ref,
    out_ref,
    grad_head_ref,
    head_rows,
    head_ref,
    logits_send,
    logits_all,
    stats_send,
    stats_all,
    head_all,
    grad_send,
    grad_all,
    pulls,
    moments,
    pair_send,
    pair_recv,
    up_send,
    up_recv,
    down_send,
    down_recv,
    logits_sems,
    stats_sems,
    head_sems,
    grad_sems,
    pair_sems,
    up_sems,
    down_sems,
):
    episodes, action_count = action_ref.shape
    rows, _ = head_ref.shape
    bins = weight_ref.shape[1]
    seq = frames_ref.shape[1]
    chunk, width = out_ref.shape
    parts, span = pair_send.shape[1], pair_send.shape[3]
    n_grp = 2 * n_out
    me, group = lax.axis_index("cp"), lax.axis_index("grp")
    place, core = group // 2, lax.rem(group, 2)
    sibling = (me, 2 * place + 1 - core)
    above, below = (me, lax.rem(group + 2, n_grp)), (me, lax.rem(group + n_grp - 2, n_grp))
    peers = [lax.rem(me + step, n_cp) for step in range(1, n_cp)]
    peers_g = [lax.rem(group + step, n_grp) for step in range(1, n_grp)]

    def to_all(send, everyone, sems, step, owner, where):
        return remote(send, everyone.at[owner], sems.at[0, step], sems.at[1, owner], where)

    lane = lax.broadcasted_iota(jnp.int32, (8, 128), 1)
    stats = jnp.zeros((8, 128), jnp.float32)
    for episode in range(episodes):
        reward, member = reward_ref[episode], id_ref[episode]
        stats = stats + jnp.where(lane == member, reward, 0.0)
        stats = stats + jnp.where(lane == group_count + member, reward * reward, 0.0)
        stats = stats + jnp.where(lane == 2 * group_count + member, 1.0, 0.0)
        for action in range(action_count):
            valid = mask_ref[episode, action].astype(jnp.float32)
            stats = stats + jnp.where(lane == 3 * group_count, valid, 0.0)
    stats_send[...] = stats
    stats_all[group] = stats
    head_rows[...] = jnp.zeros_like(head_rows)
    for episode in range(episodes):
        head_rows[episode * action_count : (episode + 1) * action_count, :] = (
            pooled_ref[episode : episode + 1, :] + embed_ref[...]
        )
    head_ref[...] = head_rows[...].astype(jnp.bfloat16)
    partial = jnp.dot(head_ref[...], weight_ref[...], preferred_element_type=jnp.float32)
    logits_send[...] = partial
    logits_all[me] = partial
    head_all[group] = head_ref[...]

    greet([(peer, group) for peer in peers] + [(me, peer) for peer in peers_g])
    for step, peer in enumerate(peers):
        to_all(logits_send, logits_all, logits_sems, step, me, (peer, group)).start()
    for step, peer in enumerate(peers_g):
        to_all(stats_send, stats_all, stats_sems, step, group, (me, peer)).start()
    for step, peer in enumerate(peers_g):
        to_all(head_ref, head_all, head_sems, step, group, (me, peer)).start()

    features = frames_ref.shape[2]
    whole, spare = divmod(features, 256)

    def moment(episode, at, down):
        moments[episode, down, :] = lax.dot_general(
            frames_ref[episode, :, at],
            slope_ref[episode],
            (((0,), (0,)), ((), ())),
            preferred_element_type=jnp.float32,
        )

    for episode in range(episodes):

        def one_tile(index, carry):
            at = pl.ds(pl.multiple_of(index * 256, 256), 256)
            moment(episode, at, at)
            return carry

        lax.fori_loop(0, whole, one_tile, 0)
        if spare:
            moment(episode, pl.ds(whole * 256, spare), pl.ds(whole * 256, spare))

    for peer in peers:
        to_all(logits_send, logits_all, logits_sems, 0, peer, (peer, group)).wait_recv()
    logits = logits_all[0]
    for slot in range(1, n_cp):
        logits = logits + logits_all[slot]
    for peer in peers_g:
        to_all(stats_send, stats_all, stats_sems, 0, peer, (me, peer)).wait_recv()
    stats = jnp.sum(stats_all[...], axis=0)[0:1]
    lane = lane[0:1]

    def entry(index):
        return jnp.sum(jnp.where(lane == index, stats, 0.0), axis=1, keepdims=True)

    mask_total = jnp.maximum(entry(3 * group_count), 1.0)
    row = lax.broadcasted_iota(jnp.int32, (rows, 1), 0)
    chosen = jnp.zeros((rows, 1), jnp.int32)
    loss_weight = jnp.zeros((rows, 1), jnp.float32)
    for episode in range(episodes):
        member = id_ref[episode]
        size = jnp.maximum(entry(2 * group_count + member), 1.0)
        mean = entry(member) / size
        variance = entry(group_count + member) / size - mean * mean
        advantage = (reward_ref[episode] - mean) / jnp.sqrt(jnp.maximum(variance, 1.0))
        for action in range(action_count):
            here = row == episode * action_count + action
            chosen = jnp.where(here, action_ref[episode, action], chosen)
            valid = mask_ref[episode, action].astype(jnp.float32)
            loss_weight = jnp.where(here, -valid * advantage / mask_total, loss_weight)
    shifted = logits - jnp.max(logits, axis=1, keepdims=True)
    log_all = shifted - jnp.log(jnp.sum(jnp.exp(shifted), axis=1, keepdims=True))
    picked = (lax.broadcasted_iota(jnp.int32, (rows, bins), 1) == chosen).astype(jnp.float32)
    logprob = jnp.sum(picked * log_all, axis=1, keepdims=True)
    logit_grad = (loss_weight * (picked - jnp.exp(log_all))).astype(jnp.bfloat16)
    pull_back = lax.dot_general(
        logit_grad, weight_ref[...], (((1,), (1,)), ((), ())), preferred_element_type=jnp.float32
    )
    for episode in range(episodes):
        mine = jnp.logical_and(row >= episode * action_count, row < (episode + 1) * action_count)
        pulls[episode : episode + 1, :] = jnp.sum(jnp.where(mine, pull_back, 0.0), axis=0, keepdims=True)
    grad_send[...] = logit_grad
    grad_all[group] = logit_grad

    block = 16 if chunk % 16 == 0 else 8

    def fill(target, slot, part, terms):
        at = pl.ds(part * span, span)
        scales = [pulls[episode : episode + 1, at] for episode in range(episodes)]

        def some(index, carry):
            here = pl.ds(pl.multiple_of(index * block, block), block)
            down = pl.ds(pl.multiple_of(slot * chunk + index * block, 8), block)
            total = moments[0, down, at] * scales[0]
            for episode in range(1, episodes):
                total = total + moments[episode, down, at] * scales[episode]
            for term in terms:
                total = total + term[here, :].astype(jnp.float32)
            target[here, :] = total.astype(jnp.bfloat16)
            return carry

        lax.fori_loop(0, chunk // block, some, 0)

    def hop(send, recv, sems, target, part, where):
        return remote(
            send.at[target, part],
            recv.at[target, part],
            sems.at[0, target, part],
            sems.at[1, target, part],
            where,
        )

    def pair_copy(target, part):
        return hop(pair_send, pair_recv, pair_sems, target, part, sibling)

    def up_copy(target, part):
        return hop(up_send, up_recv, up_sems, target, part, above)

    def down_copy(target, part):
        return hop(down_send, down_recv, down_sems, target, part, below)

    def give(target):
        for part in range(parts):
            fill(pair_send.at[target, part], 2 * target + 1 - core, part, [])
            pair_copy(target, part).start()

    last = n_out - 1
    for time in range(last):
        rising, falling = last + place - time, time - last + place

        @pl.when(time >= place)
        def _():
            give(rising)

        @pl.when(time >= last - place)
        def _():
            give(falling)

    give(place)

    for step, peer in enumerate(peers_g):
        to_all(grad_send, grad_all, grad_sems, step, group, (me, peer)).start()

    def pass_on(target, part, send, recv, copy):
        pair_copy(target, part).wait_recv()
        own = [pair_recv.at[target, part]]
        ends = place == 0 if copy is up_copy else place == last

        @pl.when(ends)
        def _():
            fill(send.at[target, part], 2 * target + core, part, own)

        @pl.when(jnp.logical_not(ends))
        def _():
            copy(target, part).wait_recv()
            fill(send.at[target, part], 2 * target + core, part, own + [recv.at[target, part]])

        copy(target, part).start()

    for time in range(last):
        rising, falling = last + place - time, time - last + place
        for part in range(parts):

            @pl.when(time >= place)
            def _():
                pass_on(rising, part, up_send, up_recv, up_copy)

            @pl.when(time >= last - place)
            def _():
                pass_on(falling, part, down_send, down_recv, down_copy)

    cell = lax.broadcasted_iota(jnp.int32, (episodes, action_count), 0) * action_count
    cell = cell + lax.broadcasted_iota(jnp.int32, (episodes, action_count), 1)
    laid = jnp.zeros((episodes, action_count), jnp.float32)
    for index in range(episodes * action_count):
        laid = jnp.where(cell == index, logprob[index : index + 1, :], laid)
    logprob_ref[...] = laid
    for peer in peers_g:
        to_all(head_ref, head_all, head_sems, 0, peer, (me, peer)).wait_recv()
        to_all(grad_send, grad_all, grad_sems, 0, peer, (me, peer)).wait_recv()
    grad_head_ref[...] = lax.dot_general(
        head_all[...].reshape(n_grp * rows, width),
        grad_all[...].reshape(n_grp * rows, bins),
        (((0,), (0,)), ((), ())),
        preferred_element_type=jnp.float32,
    ).astype(jnp.bfloat16)

    for part in range(parts):
        goal = out_ref.at[:, pl.ds(part * span, span)]
        pair_copy(place, part).wait_recv()
        own = [pair_recv.at[place, part]]
        rose, fell = up_recv.at[place, part], down_recv.at[place, part]

        @pl.when(place == 0)
        def _():
            down_copy(place, part).wait_recv()
            fill(goal, group, part, own + [fell])

        @pl.when(place == last)
        def _():
            up_copy(place, part).wait_recv()
            fill(goal, group, part, own + [rose])

        @pl.when(jnp.logical_and(place > 0, place < last))
        def _():
            up_copy(place, part).wait_recv()
            down_copy(place, part).wait_recv()
            fill(goal, group, part, own + [rose, fell])

    for target in range(n_out):
        for part in range(parts):
            pair_copy(target, part).wait_send()

            @pl.when(target > place)
            def _():
                up_copy(target, part).wait_send()

            @pl.when(target < place)
            def _():
                down_copy(target, part).wait_send()

    for step, peer in enumerate(peers):
        to_all(logits_send, logits_all, logits_sems, step, me, (peer, group)).wait_send()
    for step, peer in enumerate(peers_g):
        to_all(stats_send, stats_all, stats_sems, step, group, (me, peer)).wait_send()
        to_all(head_ref, head_all, head_sems, step, group, (me, peer)).wait_send()
        to_all(grad_send, grad_all, grad_sems, step, group, (me, peer)).wait_send()


def tail(actions, action_mask, group_ids, rewards, frames, slopes, pooled, act_embed, head_weight):
    n_cp, n_grp = lax.axis_size("cp"), lax.axis_size("grp")
    n_out = n_grp // 2
    episodes = actions.shape[0]
    group_count = max(1, episodes * n_grp // 8)
    features, width = frames.shape[2], slopes.shape[2]
    rows, bins = -(-actions.size // 16) * 16, head_weight.shape[1]
    chunk, parts = features // n_grp, 4
    in_smem = pl.BlockSpec(memory_space=pltpu.SMEM)
    in_vmem = pl.BlockSpec(memory_space=pltpu.VMEM)
    dma = pltpu.SemaphoreType.DMA
    line = pltpu.VMEM((n_out, parts, chunk, width // parts), jnp.bfloat16)
    return pl.pallas_call(
        lambda *refs: tail_kernel(n_cp, n_out, group_count, *refs),
        out_shape=(
            jax.ShapeDtypeStruct(actions.shape, jnp.float32),
            jax.ShapeDtypeStruct((chunk, width), jnp.bfloat16),
            jax.ShapeDtypeStruct((width, bins), jnp.bfloat16),
        ),
        in_specs=[in_smem] * 4 + [in_vmem] * 5,
        out_specs=(in_vmem,) * 3,
        scratch_shapes=[
            pltpu.VMEM((rows, width), jnp.float32),
            pltpu.VMEM((rows, width), jnp.bfloat16),
            pltpu.VMEM((rows, bins), jnp.float32),
            pltpu.VMEM((n_cp, rows, bins), jnp.float32),
            pltpu.VMEM((8, 128), jnp.float32),
            pltpu.VMEM((n_grp, 8, 128), jnp.float32),
            pltpu.VMEM((n_grp, rows, width), jnp.bfloat16),
            pltpu.VMEM((rows, bins), jnp.bfloat16),
            pltpu.VMEM((n_grp, rows, bins), jnp.bfloat16),
            pltpu.VMEM((-(-episodes // 8) * 8, width), jnp.float32),
            pltpu.VMEM((episodes, features, width), jnp.float32),
        ]
        + [line] * 6
        + [dma((2, n_cp))]
        + [dma((2, n_grp))] * 3
        + [dma((2, n_out, parts))] * 3,
        compiler_params=pltpu.CompilerParams(
            collective_id=1, has_side_effects=True, vmem_limit_bytes=60 * 1024 * 1024
        ),
        name="tail",
    )(actions, action_mask, group_ids, rewards, frames, slopes, pooled, act_embed, head_weight)


def front_kernel(
    n_cp,
    n_out,
    length_ref,
    query_ref,
    key_ref,
    value_ref,
    map_ref,
    shard_ref,
    frames_ref,
    columns_ref,
    scale_ref,
    heads_all,
    blocks,
    map_held,
    total,
    local_sems,
    swap_send,
    swap_recv,
    block_send,
    block_recv,
    shard_send,
    shard_recv,
    pass_send,
    pass_recv,
):
    episodes, tokens, _ = query_ref.shape
    width = blocks.shape[2]
    seq = tokens * n_cp
    n_grp = 2 * n_out
    me, group = lax.axis_index("cp"), lax.axis_index("grp")
    place, core = group // 2, lax.rem(group, 2)
    sibling = 2 * place + 1 - core
    square = n_cp == 4
    if square:
        row_peer = me + 1 - 2 * lax.rem(me, 2)
        col_peer = lax.rem(me + 2, 4)
        far_peer = lax.rem(row_peer + 2, 4)
        peers = [far_peer, row_peer, col_peer]
    else:
        peers = [lax.rem(me + step, n_cp) for step in range(1, n_cp)]
    lines = [2 * lax.rem(place + step, n_out) + core for step in range(1, n_out)]

    map_copy = pltpu.make_async_copy(map_ref, map_held, local_sems.at[0])
    map_copy.start()
    keep_copy = pltpu.make_async_copy(shard_ref, columns_ref.at[group], local_sems.at[1])
    keep_copy.start()

    def my_copy(tensor, source, episode):
        return pltpu.make_async_copy(
            source.at[episode, :, pl.ds(pl.multiple_of(me * width, 128), width)],
            heads_all.at[tensor, episode, pl.ds(pl.multiple_of(me * tokens, 8), tokens), :],
            local_sems.at[2 + tensor * episodes + episode],
        )

    def swap_copy(tensor, source, episode, step, owner, peer):
        return remote(
            source.at[episode, :, pl.ds(pl.multiple_of(peer * width, 128), width)],
            heads_all.at[tensor, episode, pl.ds(pl.multiple_of(owner * tokens, 8), tokens), :],
            swap_send.at[tensor, episode, step],
            swap_recv.at[tensor, episode, owner],
            (peer, group),
        )

    sources = (query_ref, key_ref, value_ref)
    for episode in range(episodes):
        for tensor, source in enumerate(sources):
            my_copy(tensor, source, episode).start()
    greet([(peer, group) for peer in peers] + [(me, peer) for peer in lines] + [(me, sibling)])
    for episode in range(episodes):
        for tensor, source in enumerate(sources):
            for step, peer in enumerate(peers):
                swap_copy(tensor, source, episode, step, me, peer).start()

    def shard_copy(step, owner, peer):
        return remote(shard_ref, columns_ref.at[owner], shard_send.at[step], shard_recv.at[owner], (me, peer))

    def pass_copy(step, owner, source):
        return remote(source, columns_ref.at[owner], pass_send.at[step], pass_recv.at[owner], (me, sibling))

    for step, peer in reversed(list(enumerate(lines))):
        shard_copy(step, group, peer).start()
    pass_copy(n_out - 1, group, shard_ref).start()

    def rows_of(owner, episode, first, count):
        return blocks.at[owner, pl.ds(episode * seq + first, count), :]

    def block_copy(episode, step, owner, peer, first, count, part):
        return remote(
            rows_of(owner, episode, first, count),
            rows_of(owner, episode, first, count),
            block_send.at[episode, step],
            block_recv.at[episode, owner, part],
            (peer, group),
        )

    for episode in range(episodes):
        length = jnp.full((1, seq), length_ref[episode], jnp.int32)
        kept = lax.broadcasted_iota(jnp.int32, (1, seq), 1) < length
        scale_ref[episode : episode + 1, :] = jnp.where(kept, 1.0 / length.astype(jnp.float32), 0.0)

    strip = min(seq, 256)

    def attend(episode):
        live = lax.broadcasted_iota(jnp.int32, (strip, seq), 1) < length_ref[episode]

        def one_head(head, carry):
            at = pl.ds(pl.multiple_of(head * HD, HD), HD)
            key_head = heads_all[1, episode, :, at]
            value_head = heads_all[2, episode, :, at]
            for first in range(0, seq, strip):
                query_head = heads_all[0, episode, first : first + strip, at]
                scores = lax.dot_general(
                    query_head, key_head, (((1,), (1,)), ((), ())), preferred_element_type=jnp.float32
                )
                scores = jnp.where(live, scores * (1.0 / math.sqrt(HD)), NEG_LARGE)
                probs = jnp.exp(scores - jnp.max(scores, axis=1, keepdims=True))
                row_total = jnp.sum(probs, axis=1, keepdims=True)
                weighted = jnp.dot(probs.astype(jnp.bfloat16), value_head, preferred_element_type=jnp.float32)
                blocks[me, episode * seq + first : episode * seq + first + strip, at] = (
                    weighted / row_total
                ).astype(jnp.bfloat16)
            return carry

        lax.fori_loop(0, width // HD, one_head, 0)

    def add_frames(episode, owner, opens, closes):
        tall = min(seq, 512)
        whole, spare = divmod(frames_ref.shape[2], 256)
        depth = pl.ds(pl.multiple_of(owner * width, 128), width)

        def one_tile(first, at):
            rows = pl.ds(episode * seq + first, tall)
            part = jnp.dot(blocks[owner, rows, :], map_held[depth, at], preferred_element_type=jnp.float32)
            if not opens:
                part = part + total[rows, at]
            if closes:
                frames_ref[episode, first : first + tall, at] = part.astype(jnp.bfloat16)
            else:
                total[rows, at] = part

        for first in range(0, seq, tall):

            def step(index, carry):
                one_tile(first, pl.ds(pl.multiple_of(index * 256, 256), 256))
                return carry

            lax.fori_loop(0, whole, step, 0)
            if spare:
                one_tile(first, pl.ds(whole * 256, spare))

    for episode in range(episodes):
        for tensor, source in enumerate(sources):
            my_copy(tensor, source, episode).wait()
            for peer in peers:
                swap_copy(tensor, source, episode, 0, peer, peer).wait_recv()
        attend(episode)
        if square:
            block_copy(episode, 0, me, row_peer, 0, seq, 0).start()
            block_copy(episode, 1, me, col_peer, 0, seq, 0).start()
        else:
            for step, peer in enumerate(peers):
                block_copy(episode, step, me, peer, 0, seq, 0).start()
        if episode == 0:
            map_copy.wait()
        add_frames(episode, me, True, False)

    def forward_shards():
        for step, peer in enumerate(lines):
            shard_copy(step, peer, peer).wait_recv()
            pass_copy(step, peer, columns_ref.at[peer]).start()

    half = seq // 2
    if square:
        for episode in range(episodes):
            block_copy(episode, 0, row_peer, row_peer, 0, seq, 0).wait_recv()
            block_copy(episode, 2, row_peer, col_peer, 0, half, 0).start()
            block_copy(episode, 1, col_peer, col_peer, 0, seq, 0).wait_recv()
            block_copy(episode, 3, col_peer, row_peer, half, half, 1).start()
            if episode == 0:
                forward_shards()
            add_frames(episode, row_peer, False, False)
            add_frames(episode, col_peer, False, False)
        for episode in range(episodes):
            block_copy(episode, 2, far_peer, col_peer, 0, half, 0).wait_recv()
            block_copy(episode, 3, far_peer, row_peer, half, half, 1).wait_recv()
            add_frames(episode, far_peer, False, True)
    else:
        for episode in range(episodes):
            for step, peer in enumerate(peers):
                block_copy(episode, step, peer, peer, 0, seq, 0).wait_recv()
                add_frames(episode, peer, False, step == len(peers) - 1)
        forward_shards()

    for step, peer in enumerate(lines):
        pass_copy(step, peer + 1 - 2 * core, columns_ref.at[peer]).wait_recv()
    pass_copy(n_out - 1, sibling, shard_ref).wait_recv()
    keep_copy.wait()
    for episode in range(episodes):
        for tensor, source in enumerate(sources):
            for step, peer in enumerate(peers):
                swap_copy(tensor, source, episode, step, me, peer).wait_send()
        if square:
            block_copy(episode, 0, me, row_peer, 0, seq, 0).wait_send()
            block_copy(episode, 1, me, col_peer, 0, seq, 0).wait_send()
            block_copy(episode, 2, row_peer, col_peer, 0, half, 0).wait_send()
            block_copy(episode, 3, col_peer, row_peer, half, half, 1).wait_send()
        else:
            for step, peer in enumerate(peers):
                block_copy(episode, step, me, peer, 0, seq, 0).wait_send()
    for step, peer in enumerate(lines):
        shard_copy(step, group, peer).wait_send()
        pass_copy(step, peer, columns_ref.at[peer]).wait_send()
    pass_copy(n_out - 1, group, shard_ref).wait_send()


def front(queries, keys, values, lengths, frame_map, proj_weight):
    n_cp, n_grp = lax.axis_size("cp"), lax.axis_size("grp")
    n_out = n_grp // 2
    episodes, tokens, att_width = queries.shape
    seq, width = tokens * n_cp, att_width // n_cp
    chunk, cols = proj_weight.shape
    features = frame_map.shape[1]
    anywhere = pl.BlockSpec(memory_space=pl.ANY)
    in_vmem = pl.BlockSpec(memory_space=pltpu.VMEM)
    dma = pltpu.SemaphoreType.DMA
    frames, columns, token_scale = pl.pallas_call(
        lambda *refs: front_kernel(n_cp, n_out, *refs),
        out_shape=(
            jax.ShapeDtypeStruct((episodes, seq, features), jnp.bfloat16),
            jax.ShapeDtypeStruct((n_grp, chunk, cols), jnp.bfloat16),
            jax.ShapeDtypeStruct((episodes, seq), jnp.float32),
        ),
        in_specs=[pl.BlockSpec(memory_space=pltpu.SMEM)] + [anywhere] * 4 + [in_vmem],
        out_specs=(in_vmem, anywhere, in_vmem),
        scratch_shapes=[
            pltpu.VMEM((3, episodes, seq, width), jnp.bfloat16),
            pltpu.VMEM((n_cp, episodes * seq, width), jnp.bfloat16),
            pltpu.VMEM(frame_map.shape, jnp.bfloat16),
            pltpu.VMEM((episodes * seq, features), jnp.float32),
            dma((2 + 3 * episodes,)),
            dma((3, episodes, n_cp)),
            dma((3, episodes, n_cp)),
            dma((episodes, max(n_cp, 4))),
            dma((episodes, n_cp, 2)),
            dma((n_out,)),
            dma((n_grp,)),
            dma((n_out,)),
            dma((n_grp,)),
        ],
        compiler_params=pltpu.CompilerParams(
            collective_id=3, has_side_effects=True, vmem_limit_bytes=60 * 1024 * 1024
        ),
        name="front",
    )(lengths, queries, keys, values, frame_map, proj_weight)
    return frames, columns.reshape(n_grp * chunk, cols), token_scale


def write_kernel(first, second, third, first_out, second_out, third_out):
    first_out[...] = first[...]
    second_out[...] = second[...]
    third_out[...] = third[...]


def write_out(*results):
    in_vmem = pl.BlockSpec(memory_space=pltpu.VMEM)
    return pl.pallas_call(
        write_kernel,
        out_shape=tuple(jax.ShapeDtypeStruct(result.shape, result.dtype) for result in results),
        in_specs=[in_vmem] * 3,
        out_specs=(in_vmem,) * 3,
        name="write_out",
    )(*results)


def per_device(
    queries,
    keys,
    values,
    lengths,
    frame_map,
    proj_weight,
    head_weight,
    act_embed,
    actions,
    action_mask,
    group_ids,
    rewards,
):
    episodes_here, tokens_here, att_width = queries.shape
    all_frames, proj_cols, token_scale = front(queries, keys, values, lengths, frame_map, proj_weight)
    seq_span = all_frames.shape[1]
    flat_frames = all_frames.reshape(episodes_here * seq_span, all_frames.shape[2])
    col_count = proj_cols.shape[1]
    pre_act = jnp.dot(flat_frames, proj_cols, preferred_element_type=jnp.float32).reshape(
        episodes_here, seq_span, col_count
    )
    hidden = gelu_exact(pre_act)
    pooled = jnp.sum(token_scale[:, :, None] * hidden, axis=1)
    slopes = (token_scale[:, :, None] * gelu_slope(pre_act)).astype(jnp.bfloat16)
    logprobs, grad_proj, grad_head = tail(
        actions,
        action_mask,
        group_ids,
        rewards,
        all_frames,
        slopes,
        pooled,
        act_embed,
        head_weight,
    )
    return write_out(logprobs, grad_proj, grad_head)


def solution(mesh):
    in_specs = (
        P("grp", "cp", None),
        P("grp", "cp", None),
        P("grp", "cp", None),
        P("grp"),
        P(),
        P("grp", "cp"),
        P("cp", None),
        P(None, "cp"),
        P("grp", None),
        P("grp", None),
        P("grp"),
        P("grp"),
    )
    out_specs = (P("grp", None), P("grp", "cp"), P("cp", None))
    return jax.shard_map(
        per_device, mesh=mesh, in_specs=in_specs, out_specs=out_specs, check_vma=False
    )
```
